512 devices in a mesh: row: 16 (over z_hi, y), rhs: 32 (over x, z_lo, core).
Axes of the slice: x: 4, y: 8, z: 8 (z_hi: 2, z_lo: 4; z = z_hi * 4 + z_lo), core: 2. Of those that a mesh axis runs over, the one named last changes fastest.
Arguments:
- factor: bfloat16 [2, 8192, 512], P(None, 'row', 'rhs'), may hold values from -0.25 to 0.25
- pivots: float32 [2, 512], replicated, may hold values from 2 to 3
- right_sides: float32 [8192, 4096], P('row', 'rhs'), may hold values from -6 to 6
Outputs:
- solved: float32 [8192, 4096], P('row', 'rhs')
The draws below stay inside these ranges and needn't reach their ends.
All inputs are finite; a program needn't handle non-finite values.
Results may differ from the reference program's by a relative error of at most 0.0003.
Values may be sent and summed in bfloat16 or wider, within the bound.
No kernel may reach another device: no remote copies, remote signals or barrier semaphores. Data moves between devices by JAX's collectives and lax.ppermute only.
A program may use at most 64 MiB of HBM per device.

```python
import jax
import jax.numpy as jnp
from jax import lax

NB = 512
PANELS = 2
M = 8192
RHS = 4096


def block_scale(own_key, extent, shards, smallest, top_value):
    level = 1.0
    for position, blocks in shards:
        steps = jax.random.uniform(jax.random.fold_in(jax.random.fold_in(own_key, 6), position), (blocks,), jnp.float32, smallest / len(shards), top_value / len(shards))
        level = level * jnp.repeat(jnp.exp(steps), extent[position] // blocks).reshape((-1,) + (1,) * (len(extent) - 1 - position))
    return level


def normal_values(key, shape, width, bound, pieces=(), dtype=jnp.bfloat16):
    level = block_scale(key, shape, pieces, -0.22, 0.18) if pieces else 1.0
    array = jax.random.normal(key, shape, jnp.float32) * width * level
    return jnp.minimum(jnp.maximum(array, -bound), bound).astype(dtype)


def setup_inputs(seed: int = 0) -> dict:
    arg_keys = jax.random.split(jax.random.key(seed), 4)
    return {
        "factor": normal_values(arg_keys[0], (PANELS, M, NB), (PANELS * NB * 4 // 9) ** -0.5, 0.25, ((1, 16), (2, 32))),
        "pivots": jnp.clip(jax.random.uniform(arg_keys[1], (PANELS, NB), jnp.float32, 2.0, 3.0), 2.0, 3.0),
        "right_sides": normal_values(arg_keys[2], (M, RHS), 1.0, 6.0, ((0, 16), (1, 32)), jnp.float32),
    }


def reference(factor, pivots, right_sides):
    work = right_sides.astype(jnp.float32)
    for k in range(PANELS):
        low = k * NB
        high = low + NB
        block = factor[k][low:high].astype(jnp.float32)
        diag_k = jnp.tril(block, -1) + jnp.diag(pivots[k])
        x_k = lax.linalg.triangular_solve(diag_k, work[low:high], left_side=True, lower=True)
        work = work.at[low:high].set(x_k)
        below = factor[k][high:].astype(jnp.float32)
        update = jnp.dot(below.astype(jnp.float32), x_k.astype(jnp.float32), precision=lax.Precision.HIGHEST, preferred_element_type=jnp.float32)
        work = work.at[high:].add(-update)
    return work
```

```python
import functools

import jax
import jax.numpy as jnp
from jax import lax
from jax.experimental import pallas as pl
from jax.experimental.pallas import tpu as pltpu
from jax.sharding import Mesh
from jax.sharding import PartitionSpec as P

ROW = ("zh", "y")
RHS = ("x", "zl", "c")
F32, BF16 = jnp.float32, jnp.bfloat16
BASE, BLK = 32, 128


def split2(v):
    hi = v.astype(BF16)
    lo = (v - hi.astype(F32)).astype(BF16)
    return hi, lo


def mm(a, b):
    return jnp.dot(a, b, preferred_element_type=F32)


def dot_exact_left(a, v):
    n = v.shape[1]
    both = mm(a, jnp.concatenate(split2(v), axis=1))
    return both[:, :n] + both[:, n:]


def dot_exact_right(v, b):
    m = v.shape[0]
    both = mm(jnp.concatenate(split2(v), axis=0), b)
    return both[:m] + both[m:]


def dot3(a, b):
    n = b.shape[1]
    ah, al = split2(a)
    bh, bl = split2(b)
    both = mm(ah, jnp.concatenate([bh, bl], axis=1))
    return both[:, :n] + (both[:, n:] + mm(al, bh))


def iota(shape, dim):
    return lax.broadcasted_iota(jnp.int32, shape, dim)


def invert_blocks(low, recip):
    count = len(low)
    row, lane = iota((BLK, BLK), 0), iota((BLK, BLK), 1)
    seg = lane // BASE
    packed = []
    for blk in low:
        strict = jnp.where(row > lane, blk, 0.0)
        part = jnp.zeros((BASE, BLK), F32)
        for s in range(BLK // BASE):
            part = jnp.where(seg[:BASE] == s, strict[s * BASE : (s + 1) * BASE], part)
        packed.append(part)
    packed = jnp.concatenate(packed, axis=0).astype(BF16)
    pick = row - seg * BASE
    r = [jnp.where(pick[:BASE] + seg[:BASE] * BASE == lane[:BASE] % BASE, 1.0, 0.0).astype(F32) for _ in range(count)]
    for i in range(BASE - 1):
        spread = mm(packed, jnp.where(pick == i, 1.0, 0.0).astype(BF16))
        top = (i + 1) // 8 * 8
        for k in range(count):
            x = r[k][i : i + 1] * recip[k, i : i + 1]
            tail = r[k][top:] - spread[k * BASE + top : (k + 1) * BASE] * x
            r[k] = jnp.concatenate([r[k][:top], tail], axis=0) if top else tail
    out = []
    for k in range(count):
        x = r[k] * recip[k]
        x = jnp.where(row // BASE == seg, jnp.concatenate([x] * (BLK // BASE), axis=0), 0.0)
        size = BASE
        while size < BLK:
            off = (row // size > lane // size) & (row // (2 * size) == lane // (2 * size))
            off = jnp.where(off, low[k], 0.0).astype(BF16)
            x = x - dot3(dot_exact_right(x, off), x)
            size *= 2
        out.append(x)
    return out


def substitute(inverse, lower, right):
    xs = []
    for i, inv in enumerate(inverse):
        r = right[i * BLK : (i + 1) * BLK]
        if i:
            r = r - dot_exact_left(lower(i, i), jnp.concatenate(xs, axis=0))
        xs.append(dot3(inv, r))
    return jnp.concatenate(xs, axis=0)


def first_kernel(where_ref, own_ref, other_ref, recip_ref, right_ref, panel_ref, inv_ref, x_ref, cols_ref):
    c, which = where_ref[0], where_ref[1]
    groups, count, w, rows = own_ref.shape
    width = groups * 2 * w
    for k in range(count):
        for g in range(groups):
            cols_ref[k, g, c] = own_ref[g, k]
            cols_ref[k, g, 1 - c] = other_ref[g, k]
        panel_ref[k] = cols_ref[k].reshape(width, rows).T
    low = [
        panel_ref[which, i * BLK : (i + 1) * BLK, i * BLK : (i + 1) * BLK].astype(F32) for i in range(width // BLK)
    ]
    inverse = invert_blocks(low, recip_ref[which])
    for i, inv in enumerate(inverse):
        inv_ref[i] = inv
    x_ref[...] = substitute(
        inverse, lambda i, j: panel_ref[which, i * BLK : (i + 1) * BLK, : j * BLK], right_ref[...]
    )


def second_kernel(where_ref, panel_ref, inv_ref, x0_ref, x_ref, right_ref, out_ref):
    count = inv_ref.shape[0]
    right = right_ref[...] - dot_exact_left(panel_ref[0], x0_ref[...])
    inverse = [inv_ref[i] for i in range(count)]
    x1 = substitute(inverse, lambda i, j: panel_ref[1, i * BLK : (i + 1) * BLK, : j * BLK], right)
    out_ref[...] = jnp.where(where_ref[1] == 1, x1, x_ref[...])


def last_kernel(where_ref, panel_ref, pieces_ref, x_ref, right_ref, out_ref):
    count = panel_ref.shape[0]
    width = panel_ref.shape[2]
    total = right_ref[...]
    for k in range(count):
        x = pieces_ref[:, k].reshape(width, total.shape[1])
        total = total - dot_exact_left(panel_ref[k], x)
    out_ref[...] = jnp.where(where_ref[2] < count, x_ref[...], total)


def on_chip(kernel, out_shape, n_in, scratch=()):
    vmem = pl.BlockSpec(memory_space=pltpu.VMEM)
    return pl.pallas_call(
        kernel,
        out_shape=out_shape,
        in_specs=[pl.BlockSpec(memory_space=pltpu.SMEM)] + [vmem] * (n_in - 1),
        out_specs=jax.tree.map(lambda _: vmem, out_shape),
        scratch_shapes=list(scratch),
    )


def same_to_all(piece, axes):
    count = lax.axis_size(axes)
    return lax.all_to_all(jnp.broadcast_to(piece[None], (count, *piece.shape)), axes, 0, 0, tiled=True)


def body(factor, pivots, right):
    count, rows, w = factor.shape
    width = pivots.shape[1]
    columns = right.shape[1]
    me = lax.axis_index(ROW)
    core = lax.axis_index("c")
    where = jnp.stack([core, (me == 1).astype(jnp.int32), me]).astype(jnp.int32)
    recip = (1.0 / pivots).reshape(count, width // BLK, BLK // BASE, BASE)
    recip = jnp.repeat(jnp.swapaxes(recip, 2, 3), BASE, axis=3)

    piece = jnp.swapaxes(factor, 1, 2)
    near = same_to_all(piece, "zl")
    own = same_to_all(near, "x")
    own = own.reshape(-1, count, w, rows)
    other = lax.ppermute(own, "c", [(0, 1), (1, 0)])

    panel, inv, x = on_chip(
        first_kernel,
        (
            jax.ShapeDtypeStruct((count, rows, width), BF16),
            jax.ShapeDtypeStruct((width // BLK, BLK, BLK), F32),
            jax.ShapeDtypeStruct((rows, columns), F32),
        ),
        5,
        [pltpu.VMEM((count, own.shape[0], 2, w, rows), BF16)],
    )(where, own, other, recip, right)
    x0 = lax.ppermute(x, "y", [(0, 1)])
    out = jax.ShapeDtypeStruct((rows, columns), F32)
    x = on_chip(second_kernel, out, 6)(where, panel, inv, x0, x, right)
    n = lax.axis_size(ROW)
    mine = lax.all_to_all(x.reshape(n, rows // n, columns), ROW, 0, 0, tiled=True)[:count]
    pieces = same_to_all(mine, ROW)
    return on_chip(last_kernel, out, 5)(where, panel, pieces, x, right)


def solution(mesh):
    ids = mesh.devices
    shape = (2, ids.shape[0] // 2, ids.shape[1] // 8, 4, 2)
    split = Mesh(ids.reshape(shape), ROW + RHS)
    return jax.shard_map(
        body,
        mesh=split,
        in_specs=(P(None, ROW, RHS), P(), P(ROW, RHS)),
        out_specs=P(ROW, RHS),
        check_vma=False,
    )
```

```python
import jax
import jax.numpy as jnp
from jax import lax
from jax.experimental import pallas as pl
from jax.experimental.pallas import tpu as pltpu
from jax.sharding import Mesh
from jax.sharding import PartitionSpec as P


ROW = ("zh", "yh", "yl")
RHS = ("x", "zl", "c")
F32, BF16 = jnp.float32, jnp.bfloat16
BASE, BLK, BIG = 32, 128, 256
SPAN = 14.0


def split2(v):
    hi = v.astype(BF16)
    lo = (v - hi.astype(F32)).astype(BF16)
    return hi, lo


def mm(a, b, trans=False):
    return lax.dot_general(a, b, (((1,), (1 if trans else 0,)), ((), ())), preferred_element_type=F32)


def dot_exact_left(a, v):
    n = v.shape[1]
    both = mm(a, jnp.concatenate(split2(v), axis=1))
    return both[:, :n] + both[:, n:]


def dot_exact_right(v, b):
    m = v.shape[0]
    both = mm(jnp.concatenate(split2(v), axis=0), b)
    return both[:m] + both[m:]


def dot3(a, b, trans=False):
    m = a.shape[0]
    ah, al = split2(a)
    bh, bl = split2(b)
    both = mm(jnp.concatenate([ah, al], axis=0), bh, trans)
    return both[:m] + (both[m:] + mm(ah, bl, trans))


def iota(shape, dim):
    return lax.broadcasted_iota(jnp.int32, shape, dim)


def spread_recip(pivot, row, seg):
    lane = iota((BASE, BLK), 1)
    left = jnp.where(lane % BASE == iota((BASE, BLK), 0), pivot, 0.0)
    same = jnp.where(row // BASE == seg, 1.0, 0.0).astype(BF16)
    a, rest = split2(left)
    b = rest
    c = (left - a.astype(F32) - b.astype(F32)).astype(BF16)
    got = mm(jnp.concatenate([a, b, c], axis=0), same)
    return 1.0 / (got[:BASE] + got[BASE : 2 * BASE] + got[2 * BASE :])


def invert_blocks(low, pivot):
    count = len(low)
    row, lane = iota((BLK, BLK), 0), iota((BLK, BLK), 1)
    seg = lane // BASE
    recip = [spread_recip(p, row, seg) for p in pivot]
    packed = []
    for blk in low:
        strict = jnp.where(row > lane, blk, 0.0)
        part = strict[:BASE]
        for s in range(1, BLK // BASE):
            part = jnp.where(seg[:BASE] == s, strict[s * BASE : (s + 1) * BASE], part)
        packed.append(part)
    packed = jnp.concatenate(packed, axis=0).astype(BF16)
    pick = row - seg * BASE
    one = jnp.where(row[:BASE] == lane[:BASE] % BASE, 1.0, 0.0).astype(F32)
    r = [one] * count
    for i in range(BASE - 1):
        spread = mm(packed, jnp.where(pick == i, 1.0, 0.0).astype(BF16))
        top = (i + 1) // 8 * 8
        for k in range(count):
            x = r[k][i : i + 1] * recip[k][i : i + 1]
            tail = r[k][top:] - spread[k * BASE + top : (k + 1) * BASE] * x
            r[k] = jnp.concatenate([r[k][:top], tail], axis=0) if top else tail
    out = []
    for k in range(count):
        x = r[k] * recip[k]
        out.append(jnp.where(row // BASE == seg, jnp.concatenate([x] * (BLK // BASE), axis=0), 0.0))
    size = BASE
    while size < BLK:
        off = (row // size > lane // size) & (row // (2 * size) == lane // (2 * size))
        half = [dot_exact_right(x, jnp.where(off, blk, 0.0).astype(BF16)) for x, blk in zip(out, low)]
        out = [x - dot3(h, x) for x, h in zip(out, half)]
        size *= 2
    return out


def join_blocks(first, second, low):
    off = -dot3(second, dot_exact_left(low, first))
    top = jnp.concatenate([first, jnp.zeros_like(first)], axis=1)
    return jnp.concatenate([top, jnp.concatenate([off, second], axis=1)], axis=0)


def substitute(inverse, upper, right):
    xs = []
    for j, inv in enumerate(inverse):
        r = right[:, j * BIG : (j + 1) * BIG]
        if j:
            r = r - dot_exact_right(jnp.concatenate(xs, axis=1), upper(j * BIG, j))
        xs.append(dot3(r, inv, trans=True))
    return jnp.concatenate(xs, axis=1)


def scaled(x):
    largest = jnp.max(jnp.abs(x), axis=1, keepdims=True)
    power = jnp.clip(jnp.ceil(jnp.log2(largest)), -100.0, 127.0)
    return jnp.concatenate([x * jnp.exp2(SPAN - power), jnp.broadcast_to(power, (x.shape[0], BLK))], axis=1)


def solve_kernel(
    where_ref, own_ref, other_ref, pivot_ref, first_ref, right_ref, x_ref, sent_ref, panel_ref, top_ref
):
    me, core = where_ref[0], where_ref[1]
    groups, panels, w, _ = own_ref.shape
    for k in range(panels):
        into = top_ref if k == panels - 1 else panel_ref.at[k]
        for g in range(groups):
            into[pl.ds(pl.multiple_of((2 * g + core) * w, w), w)] = own_ref[g, k]
            into[pl.ds(pl.multiple_of((2 * g + 1 - core) * w, w), w)] = other_ref[g, k]
    width = 2 * groups * w
    blocks = width // BLK
    low, pivot = [], []
    for k, ref in enumerate((top_ref, panel_ref.at[1])):
        for i in range(blocks):
            s = slice(i * BLK, (i + 1) * BLK)
            low.append(ref[s, s].astype(F32).T)
            pivot.append(pivot_ref[k : k + 1, s])
    small = invert_blocks(low, pivot)
    inverse = []
    for k, ref in enumerate((top_ref, panel_ref.at[1])):
        for i in range(0, blocks, 2):
            at = i * BLK
            sub = ref[at : at + BLK, at + BLK : at + 2 * BLK].astype(F32).T.astype(BF16)
            inverse.append(join_blocks(small[k * blocks + i], small[k * blocks + i + 1], sub))
    half = len(inverse) // 2
    right = right_ref[...].T
    b0 = jnp.where(me == 0, right, first_ref[...].T)
    x0 = substitute(inverse[:half], lambda n, j: top_ref[:n, j * BIG : (j + 1) * BIG], b0)
    r1 = right - dot_exact_right(x0, panel_ref[0])
    x1 = substitute(inverse[half:], lambda n, j: panel_ref[1, :n, j * BIG : (j + 1) * BIG], r1)
    x = jnp.where(me == 0, x0, x1)
    x_ref[...] = x
    sent_ref[...] = scaled(x)


def last_kernel(where_ref, panel_ref, pieces_ref, x_ref, right_ref, out_ref):
    count, width, _ = panel_ref.shape
    columns = x_ref.shape[0]
    update = 0.0
    for k in range(count):
        got = pieces_ref[:, k].reshape(columns, width + BLK)
        term = dot_exact_right(got[:, :width], panel_ref[k])
        update = update + term * jnp.exp2(got[:, width : width + 1] - SPAN)
    solved = where_ref[0] < count
    turned = jnp.where(solved, x_ref[...], update).T
    out_ref[...] = jnp.where(solved, turned, right_ref[...] - turned)


def on_chip(kernel, out_shape, n_in, scratch=()):
    vmem = pl.BlockSpec(memory_space=pltpu.VMEM)
    return pl.pallas_call(
        kernel,
        out_shape=out_shape,
        in_specs=[pl.BlockSpec(memory_space=pltpu.SMEM)] + [vmem] * (n_in - 1),
        out_specs=jax.tree.map(lambda _: vmem, out_shape),
        scratch_shapes=list(scratch),
        compiler_params=pltpu.CompilerParams(vmem_limit_bytes=24 * 1024 * 1024),
    )


def same_to_all(piece, axes):
    count = lax.axis_size(axes)
    return lax.all_to_all(jnp.broadcast_to(piece[None], (count, *piece.shape)), axes, 0, 0, tiled=True)


def whole(factor, pivots, right):
    count, rows, w = factor.shape
    width = pivots.shape[1]
    columns = right.shape[1]
    where = jnp.stack([lax.axis_index(ROW), lax.axis_index("c")]).astype(jnp.int32)
    n = lax.axis_size(ROW)

    piece = jnp.swapaxes(factor, 1, 2)
    both = same_to_all(piece, ("yl", "zl"))
    both = both.reshape(2, -1, count, w, rows)
    first = lax.ppermute(right, "yl", [(0, 1)])
    own = jnp.where(lax.axis_index("yl") == 0, both[0], both[1])
    cols = jnp.concatenate([own, both[0][:, :1]], axis=1)
    cols = lax.all_gather(cols, "x", axis=0, tiled=True)
    other = lax.ppermute(cols, "c", [(0, 1), (1, 0)])

    x, sent, panel = on_chip(
        solve_kernel,
        (
            jax.ShapeDtypeStruct((columns, width), F32),
            jax.ShapeDtypeStruct((columns, width + BLK), F32),
            jax.ShapeDtypeStruct((count, width, rows), BF16),
        ),
        6,
        [pltpu.VMEM((width, rows), BF16)],
    )(where, cols, other, pivots, first, right)
    sent = sent.astype(jnp.float16).reshape(n, columns // n, width + BLK)
    mine = lax.all_to_all(sent, ROW, 0, 0, tiled=True)[:count]
    pieces = same_to_all(mine, ROW).astype(F32)
    return on_chip(last_kernel, jax.ShapeDtypeStruct((rows, columns), F32), 5)(where, panel, pieces, x, right)


def solution(mesh):
    ids = mesh.devices
    shape = (2, ids.shape[0] // 4, 2, ids.shape[1] // 8, 4, 2)
    split = Mesh(ids.reshape(shape), ROW + RHS)
    return jax.shard_map(
        whole,
        mesh=split,
        in_specs=(P(None, ROW, RHS), P(), P(ROW, RHS)),
        out_specs=P(ROW, RHS),
        check_vma=False,
    )
```

```python
import jax
import jax.numpy as jnp
from jax import lax
from jax.experimental import pallas as pl
from jax.experimental.pallas import tpu as pltpu
from jax.sharding import Mesh
from jax.sharding import PartitionSpec as P

ROW = ("zh", "yh", "yl")
RHS = ("x", "zl", "c")
F32, BF16 = jnp.float32, jnp.bfloat16
BASE, BLK, BIG = 32, 128, 256
SPAN = 14.0


def split2(v):
    hi = v.astype(BF16)
    lo = (v - hi.astype(F32)).astype(BF16)
    return hi, lo


def mm(a, b, trans=False):
    return lax.dot_general(a, b, (((1,), (1 if trans else 0,)), ((), ())), preferred_element_type=F32)


def dot_exact_left(a, v):
    n = v.shape[1]
    both = mm(a, jnp.concatenate(split2(v), axis=1))
    return both[:, :n] + both[:, n:]


def dot_exact_right(v, b):
    m = v.shape[0]
    both = mm(jnp.concatenate(split2(v), axis=0), b)
    return both[:m] + both[m:]


def dot3(a, b, trans=False):
    m = a.shape[0]
    ah, al = split2(a)
    bh, bl = split2(b)
    both = mm(jnp.concatenate([ah, al], axis=0), bh, trans)
    return both[:m] + (both[m:] + mm(ah, bl, trans))


def iota(shape, dim):
    return lax.broadcasted_iota(jnp.int32, shape, dim)


def spread_recip(pivot, row, seg):
    lane = iota((BASE, BLK), 1)
    left = jnp.where(lane % BASE == iota((BASE, BLK), 0), pivot, 0.0)
    same = jnp.where(row // BASE == seg, 1.0, 0.0).astype(BF16)
    a, rest = split2(left)
    b = rest
    c = (left - a.astype(F32) - b.astype(F32)).astype(BF16)
    got = mm(jnp.concatenate([a, b, c], axis=0), same)
    return 1.0 / (got[:BASE] + got[BASE : 2 * BASE] + got[2 * BASE :])


def invert_blocks(low, pivot):
    count = len(low)
    row, lane = iota((BLK, BLK), 0), iota((BLK, BLK), 1)
    seg = lane // BASE
    recip = [spread_recip(p, row, seg) for p in pivot]
    packed = []
    for blk in low:
        strict = jnp.where(row > lane, blk, 0.0)
        part = strict[:BASE]
        for s in range(1, BLK // BASE):
            part = jnp.where(seg[:BASE] == s, strict[s * BASE : (s + 1) * BASE], part)
        packed.append(part)
    packed = jnp.concatenate(packed, axis=0).astype(BF16)
    pick = row - seg * BASE
    one = jnp.where(row[:BASE] == lane[:BASE] % BASE, 1.0, 0.0).astype(F32)
    r = [one] * count
    for i in range(BASE - 1):
        spread = mm(packed, jnp.where(pick == i, 1.0, 0.0).astype(BF16))
        top = (i + 1) // 8 * 8
        for k in range(count):
            x = r[k][i : i + 1] * recip[k][i : i + 1]
            tail = r[k][top:] - spread[k * BASE + top : (k + 1) * BASE] * x
            r[k] = jnp.concatenate([r[k][:top], tail], axis=0) if top else tail
    out = []
    for k in range(count):
        x = r[k] * recip[k]
        out.append(jnp.where(row // BASE == seg, jnp.concatenate([x] * (BLK // BASE), axis=0), 0.0))
    size = BASE
    while size < BLK:
        off = (row // size > lane // size) & (row // (2 * size) == lane // (2 * size))
        half = [dot_exact_right(x, jnp.where(off, blk, 0.0).astype(BF16)) for x, blk in zip(out, low)]
        out = [x - dot3(h, x) for x, h in zip(out, half)]
        size *= 2
    return out


def join_blocks(first, second, low):
    off = -dot3(second, dot_exact_left(low, first))
    top = jnp.concatenate([first, jnp.zeros_like(first)], axis=1)
    return jnp.concatenate([top, jnp.concatenate([off, second], axis=1)], axis=0)


def substitute(inverse, upper, right):
    xs = []
    for j, inv in enumerate(inverse):
        r = right[:, j * BIG : (j + 1) * BIG]
        if j:
            r = r - dot_exact_right(jnp.concatenate(xs, axis=1), upper(j * BIG, j))
        xs.append(dot3(r, inv, trans=True))
    return jnp.concatenate(xs, axis=1)


def scaled(x):
    largest = jnp.max(jnp.abs(x), axis=1, keepdims=True)
    power = jnp.clip(jnp.ceil(jnp.log2(largest)), -100.0, 127.0)
    return jnp.concatenate([x * jnp.exp2(SPAN - power), jnp.broadcast_to(power, (x.shape[0], BLK))], axis=1)


def first_kernel(where_ref, own_ref, other_ref, pivot_ref, right_ref, x_ref, sent_ref, inv_ref, panel_ref):
    me, core = where_ref[0], where_ref[1]
    groups, count, w, rows = own_ref.shape
    for k in range(count):
        into = panel_ref.at[k]
        for g in range(groups):
            into[pl.ds(pl.multiple_of((2 * g + core) * w, w), w)] = own_ref[g, k]
            into[pl.ds(pl.multiple_of((2 * g + 1 - core) * w, w), w)] = other_ref[g, k]

    @pl.when(me < count)
    def _():
        blocks = 2 * groups * w // BLK
        low, pivot = [], []
        for i in range(blocks):
            s = slice(i * BLK, (i + 1) * BLK)
            low.append(panel_ref[me, s, s].astype(F32).T)
            pivot.append(jnp.where(me == 0, pivot_ref[0:1, s], pivot_ref[1:2, s]))
        small = invert_blocks(low, pivot)
        inverse = []
        for i in range(0, blocks, 2):
            at = i * BLK
            sub = panel_ref[me, at : at + BLK, at + BLK : at + 2 * BLK].astype(F32).T.astype(BF16)
            inverse.append(join_blocks(small[i], small[i + 1], sub))
            inv_ref[i // 2] = inverse[-1]
        x = substitute(inverse, lambda n, j: panel_ref[me, :n, j * BIG : (j + 1) * BIG], right_ref[...].T)
        x_ref[...] = x
        sent_ref[...] = scaled(x)


def unscaled(got):
    return got[:, :-BLK] * jnp.exp2(got[:, -BLK : 1 - BLK] - SPAN)


def second_kernel(where_ref, got_ref, panel_ref, inv_ref, right_ref, x_ref, sent_ref, out_ref, out_sent_ref):
    me = where_ref[0]

    @pl.when(me == 0)
    def _():
        out_ref[...] = x_ref[...]
        out_sent_ref[...] = sent_ref[...]

    @pl.when(me == 1)
    def _():
        inverse = [inv_ref[i] for i in range(inv_ref.shape[0])]
        right = right_ref[...].T - dot_exact_right(unscaled(got_ref[...]), panel_ref[0])
        x = substitute(inverse, lambda n, j: panel_ref[1, :n, j * BIG : (j + 1) * BIG], right)
        out_ref[...] = x
        out_sent_ref[...] = scaled(x)


def last_kernel(where_ref, panel_ref, pieces_ref, x_ref, right_ref, out_ref):
    count, width, _ = panel_ref.shape
    columns = x_ref.shape[0]
    update = 0.0
    for k in range(count):
        got = pieces_ref[:, k].reshape(columns, width + BLK)
        update = update + dot_exact_right(unscaled(got), panel_ref[k])
    solved = where_ref[0] < count
    turned = jnp.where(solved, x_ref[...], update).T
    out_ref[...] = jnp.where(solved, turned, right_ref[...] - turned)


def on_chip(kernel, out_shape, n_in, scratch=()):
    vmem = pl.BlockSpec(memory_space=pltpu.VMEM)
    return pl.pallas_call(
        kernel,
        out_shape=out_shape,
        in_specs=[pl.BlockSpec(memory_space=pltpu.SMEM)] + [vmem] * (n_in - 1),
        out_specs=jax.tree.map(lambda _: vmem, out_shape),
        scratch_shapes=list(scratch),
        compiler_params=pltpu.CompilerParams(vmem_limit_bytes=24 * 1024 * 1024),
    )


def same_to_all(piece, axes):
    count = lax.axis_size(axes)
    return lax.all_to_all(jnp.broadcast_to(piece[None], (count, *piece.shape)), axes, 0, 0, tiled=True)


def body(factor, pivots, right):
    count, rows, w = factor.shape
    width = pivots.shape[1]
    columns = right.shape[1]
    where = jnp.stack([lax.axis_index(ROW), lax.axis_index("c")]).astype(jnp.int32)
    n = lax.axis_size(ROW)

    piece = jnp.swapaxes(factor, 1, 2)
    own = same_to_all(same_to_all(piece, "zl"), "x").reshape(-1, count, w, rows)
    other = lax.ppermute(own, "c", [(0, 1), (1, 0)])

    solved = (jax.ShapeDtypeStruct((columns, width), F32), jax.ShapeDtypeStruct((columns, width + BLK), F32))
    kept = (jax.ShapeDtypeStruct((width // BIG, BIG, BIG), F32), jax.ShapeDtypeStruct((count, width, rows), BF16))
    x, sent, inverse, panel = on_chip(first_kernel, solved + kept, 5)(where, own, other, pivots, right)
    got = lax.ppermute(sent.astype(jnp.float16), ROW, [(0, 1)]).astype(F32)
    x, sent = on_chip(second_kernel, solved, 7)(where, got, panel, inverse, right, x, sent)
    sent = sent.astype(jnp.float16).reshape(n, columns // n, width + BLK)
    mine = lax.all_to_all(sent, ROW, 0, 0, tiled=True)[:count]
    pieces = same_to_all(mine, ROW).astype(F32)
    return on_chip(last_kernel, jax.ShapeDtypeStruct((rows, columns), F32), 5)(where, panel, pieces, x, right)


def solution(mesh):
    ids = mesh.devices
    shape = (2, ids.shape[0] // 4, 2, ids.shape[1] // 8, 4, 2)
    split = Mesh(ids.reshape(shape), ROW + RHS)
    return jax.shard_map(
        body,
        mesh=split,
        in_specs=(P(None, ROW, RHS), P(), P(ROW, RHS)),
        out_specs=P(ROW, RHS),
        check_vma=False,
    )
```

```python
import jax
import jax.numpy as jnp
from jax import lax
from jax.experimental import pallas as pl
from jax.experimental.pallas import tpu as pltpu
from jax.sharding import Mesh
from jax.sharding import PartitionSpec as P


ROW = ("zh", "yh", "yl")
RHS = ("x", "zl", "c")
F32, BF16 = jnp.float32, jnp.bfloat16
BASE, BLK, BIG = 32, 128, 256
SPAN = 14.0


def split2(v):
    hi = v.astype(BF16)
    lo = (v - hi.astype(F32)).astype(BF16)
    return hi, lo


def mm(a, b, trans=False):
    return lax.dot_general(a, b, (((1,), (1 if trans else 0,)), ((), ())), preferred_element_type=F32)


def dot_exact_left(a, v):
    n = v.shape[1]
    both = mm(a, jnp.concatenate(split2(v), axis=1))
    return both[:, :n] + both[:, n:]


def dot_exact_right(v, b):
    m = v.shape[0]
    both = mm(jnp.concatenate(split2(v), axis=0), b)
    return both[:m] + both[m:]


def dot3(a, b, trans=False):
    m = a.shape[0]
    ah, al = split2(a)
    bh, bl = split2(b)
    both = mm(jnp.concatenate([ah, al], axis=0), bh, trans)
    return both[:m] + (both[m:] + mm(ah, bl, trans))


def iota(shape, dim):
    return lax.broadcasted_iota(jnp.int32, shape, dim)


def spread_recip(pivot, row, seg):
    lane = iota((BASE, BLK), 1)
    left = jnp.where(lane % BASE == iota((BASE, BLK), 0), pivot, 0.0)
    same = jnp.where(row // BASE == seg, 1.0, 0.0).astype(BF16)
    a, rest = split2(left)
    b = rest
    c = (left - a.astype(F32) - b.astype(F32)).astype(BF16)
    got = mm(jnp.concatenate([a, b, c], axis=0), same)
    return 1.0 / (got[:BASE] + got[BASE : 2 * BASE] + got[2 * BASE :])


def invert_blocks(low, pivot):
    count = len(low)
    row, lane = iota((BLK, BLK), 0), iota((BLK, BLK), 1)
    seg = lane // BASE
    recip = [spread_recip(p, row, seg) for p in pivot]
    packed = []
    for blk in low:
        strict = jnp.where(row > lane, blk, 0.0)
        part = strict[:BASE]
        for s in range(1, BLK // BASE):
            part = jnp.where(seg[:BASE] == s, strict[s * BASE : (s + 1) * BASE], part)
        packed.append(part)
    packed = jnp.concatenate(packed, axis=0).astype(BF16)
    pick = row - seg * BASE
    one = jnp.where(row[:BASE] == lane[:BASE] % BASE, 1.0, 0.0).astype(F32)
    r = [one] * count
    for i in range(BASE - 1):
        spread = mm(packed, jnp.where(pick == i, 1.0, 0.0).astype(BF16))
        top = (i + 1) // 8 * 8
        for k in range(count):
            x = r[k][i : i + 1] * recip[k][i : i + 1]
            tail = r[k][top:] - spread[k * BASE + top : (k + 1) * BASE] * x
            r[k] = jnp.concatenate([r[k][:top], tail], axis=0) if top else tail
    out = []
    for k in range(count):
        x = r[k] * recip[k]
        out.append(jnp.where(row // BASE == seg, jnp.concatenate([x] * (BLK // BASE), axis=0), 0.0))
    size = BASE
    while size < BLK:
        off = (row // size > lane // size) & (row // (2 * size) == lane // (2 * size))
        half = [dot_exact_right(x, jnp.where(off, blk, 0.0).astype(BF16)) for x, blk in zip(out, low)]
        out = [x - dot3(h, x) for x, h in zip(out, half)]
        size *= 2
    return out


def join_blocks(first, second, low):
    off = -dot3(second, dot_exact_left(low, first))
    top = jnp.concatenate([first, jnp.zeros_like(first)], axis=1)
    return jnp.concatenate([top, jnp.concatenate([off, second], axis=1)], axis=0)


def substitute(inverse, upper, right):
    xs = []
    for j, inv in enumerate(inverse):
        r = right[:, j * BIG : (j + 1) * BIG]
        if j:
            r = r - dot_exact_right(jnp.concatenate(xs, axis=1), upper(j * BIG, j))
        xs.append(dot3(r, inv, trans=True))
    return jnp.concatenate(xs, axis=1)


def scaled(x):
    largest = jnp.max(jnp.abs(x), axis=1, keepdims=True)
    power = jnp.clip(jnp.ceil(jnp.log2(largest)), -100.0, 127.0)
    return jnp.concatenate([x * jnp.exp2(SPAN - power), jnp.broadcast_to(power, (x.shape[0], BLK))], axis=1)


def invert_panel(panel, pivot):
    blocks = pivot.shape[1] // BLK
    at = [slice(i * BLK, (i + 1) * BLK) for i in range(blocks)]
    small = invert_blocks([panel[s, s].astype(F32).T for s in at], [pivot[:, s] for s in at])
    return [
        join_blocks(small[i], small[i + 1], panel[at[i], at[i + 1]].astype(F32).T.astype(BF16))
        for i in range(0, blocks, 2)
    ]


def first_kernel(own_ref, other_ref, pivot_ref, right_ref, x_ref, sent_ref, panel_ref):
    me, core = lax.axis_index(ROW), lax.axis_index("c")
    groups, count, w, _ = own_ref.shape
    for k in range(count):
        into = panel_ref.at[k]
        for g in range(groups):
            into[pl.ds(pl.multiple_of((2 * g + core) * w, w), w)] = own_ref[g, k]
            into[pl.ds(pl.multiple_of((2 * g + 1 - core) * w, w), w)] = other_ref[g, k]

    @pl.when(me == 0)
    def _():
        inverse = invert_panel(panel_ref.at[0], pivot_ref[0:1])
        x = substitute(inverse, lambda n, j: panel_ref[0, :n, j * BIG : (j + 1) * BIG], right_ref[...].T)
        x_ref[...] = x
        sent_ref[...] = scaled(x)


def invert_kernel(panel_ref, pivot_ref, right_ref, inv_ref, turned_ref):
    @pl.when(lax.axis_index(ROW) == 1)
    def _():
        turned_ref[...] = right_ref[...].T
        for i, inv in enumerate(invert_panel(panel_ref.at[1], pivot_ref[1:2])):
            inv_ref[i] = inv


def unscaled(got):
    return got[:, :-BLK] * jnp.exp2(got[:, -BLK : 1 - BLK] - SPAN)


def second_kernel(got_ref, panel_ref, inv_ref, turned_ref, x_ref, sent_ref, out_ref, out_sent_ref):
    me = lax.axis_index(ROW)

    @pl.when(me == 0)
    def _():
        out_ref[...] = x_ref[...]
        out_sent_ref[...] = sent_ref[...]

    @pl.when(me == 1)
    def _():
        inverse = [inv_ref[i] for i in range(inv_ref.shape[0])]
        right = turned_ref[...] - dot_exact_right(unscaled(got_ref[...]), panel_ref[0])
        x = substitute(inverse, lambda n, j: panel_ref[1, :n, j * BIG : (j + 1) * BIG], right)
        out_ref[...] = x
        out_sent_ref[...] = scaled(x)


def last_kernel(panel_ref, pieces_ref, x_ref, right_ref, out_ref):
    count, width, _ = panel_ref.shape
    columns = x_ref.shape[0]
    got = pieces_ref[...].reshape(columns, count * width + BLK)
    update = 0.0
    for k in range(count):
        at = count * width + k * BLK // count
        x = got[:, k * width : (k + 1) * width] * jnp.exp2(got[:, at : at + 1] - SPAN)
        update = update + dot_exact_right(x, panel_ref[k])
    solved = lax.axis_index(ROW) < count
    turned = jnp.where(solved, x_ref[...], update).T
    out_ref[...] = jnp.where(solved, turned, right_ref[...] - turned)


def on_chip(kernel, out_shape, n_in, scratch=()):
    vmem = pl.BlockSpec(memory_space=pltpu.VMEM)
    return pl.pallas_call(
        kernel,
        out_shape=out_shape,
        in_specs=[vmem] * n_in,
        out_specs=jax.tree.map(lambda _: vmem, out_shape),
        scratch_shapes=list(scratch),
        compiler_params=pltpu.CompilerParams(vmem_limit_bytes=24 * 1024 * 1024),
    )


def same_to_all(piece, axes):
    count = lax.axis_size(axes)
    return lax.all_to_all(jnp.broadcast_to(piece[None], (count, *piece.shape)), axes, 0, 0, tiled=True)


def whole(factor, pivots, right):
    count, rows, w = factor.shape
    width = pivots.shape[1]
    columns = right.shape[1]
    n = lax.axis_size(ROW)

    piece = jnp.swapaxes(factor, 1, 2)
    own = same_to_all(same_to_all(piece, "zl"), "x").reshape(-1, count, w, rows)
    other = lax.ppermute(own, "c", [(0, 1), (1, 0)])

    solved = (jax.ShapeDtypeStruct((columns, width), F32), jax.ShapeDtypeStruct((columns, width + BLK), F32))
    all_cols = (jax.ShapeDtypeStruct((count, width, rows), BF16),)
    kept = (jax.ShapeDtypeStruct((width // BIG, BIG, BIG), F32), jax.ShapeDtypeStruct((columns, width), F32))
    x, sent, panel = on_chip(first_kernel, solved + all_cols, 4)(own, other, pivots, right)
    got = lax.ppermute(sent.astype(jnp.float16), ROW, [(0, 1)])
    inverse, turned = on_chip(invert_kernel, kept, 3)(panel, pivots, right)
    x, sent = on_chip(second_kernel, solved, 6)(got.astype(F32), panel, inverse, turned, x, sent)
    sent = sent.astype(jnp.float16).reshape(n, columns // n, width + BLK)
    mine = lax.all_to_all(sent, ROW, 0, 0, tiled=True)[:count]
    share = BLK // count
    power = [mine[k, :, width + k * share : width + (k + 1) * share] for k in range(count)]
    mine = jnp.concatenate([mine[k, :, :width] for k in range(count)] + power, axis=1)
    pieces = same_to_all(mine, ROW).astype(F32)
    return on_chip(last_kernel, jax.ShapeDtypeStruct((rows, columns), F32), 4)(panel, pieces, x, right)


def solution(mesh):
    ids = mesh.devices
    shape = (2, ids.shape[0] // 4, 2, ids.shape[1] // 8, 4, 2)
    split = Mesh(ids.reshape(shape), ROW + RHS)
    return jax.shard_map(
        whole,
        mesh=split,
        in_specs=(P(None, ROW, RHS), P(), P(ROW, RHS)),
        out_specs=P(ROW, RHS),
        check_vma=False,
    )
```

```python
import jax
import jax.numpy as jnp
from jax import lax
from jax.experimental import pallas as pl
from jax.experimental.pallas import tpu as pltpu
from jax.sharding import Mesh
from jax.sharding import PartitionSpec as P


ROW = ("zh", "yh", "yl")
RHS = ("x", "zl", "c")
F32, BF16 = jnp.float32, jnp.bfloat16
BASE, BLK, BIG = 32, 128, 256
SPAN = 14.0


def split2(v):
    hi = v.astype(BF16)
    lo = (v - hi.astype(F32)).astype(BF16)
    return hi, lo


def mm(a, b, trans=False):
    return lax.dot_general(a, b, (((1,), (1 if trans else 0,)), ((), ())), preferred_element_type=F32)


def dot_exact_left(a, v):
    n = v.shape[1]
    both = mm(a, jnp.concatenate(split2(v), axis=1))
    return both[:, :n] + both[:, n:]


def dot_exact_right(v, b):
    m = v.shape[0]
    both = mm(jnp.concatenate(split2(v), axis=0), b)
    return both[:m] + both[m:]


def dot3(a, b, trans=False):
    m = a.shape[0]
    ah, al = split2(a)
    bh, bl = split2(b)
    both = mm(jnp.concatenate([ah, al], axis=0), bh, trans)
    return both[:m] + (both[m:] + mm(ah, bl, trans))


def iota(shape, dim):
    return lax.broadcasted_iota(jnp.int32, shape, dim)


def spread_recip(pivot, row, seg):
    lane = iota((BASE, BLK), 1)
    left = jnp.where(lane % BASE == iota((BASE, BLK), 0), pivot, 0.0)
    same = jnp.where(row // BASE == seg, 1.0, 0.0).astype(BF16)
    a, rest = split2(left)
    b = rest
    c = (left - a.astype(F32) - b.astype(F32)).astype(BF16)
    got = mm(jnp.concatenate([a, b, c], axis=0), same)
    return 1.0 / (got[:BASE] + got[BASE : 2 * BASE] + got[2 * BASE :])


def invert_blocks(low, pivot):
    count = len(low)
    row, lane = iota((BLK, BLK), 0), iota((BLK, BLK), 1)
    seg = lane // BASE
    recip = [spread_recip(p, row, seg) for p in pivot]
    packed = []
    for blk in low:
        strict = jnp.where(row > lane, blk, 0.0)
        part = strict[:BASE]
        for s in range(1, BLK // BASE):
            part = jnp.where(seg[:BASE] == s, strict[s * BASE : (s + 1) * BASE], part)
        packed.append(part)
    packed = jnp.concatenate(packed, axis=0).astype(BF16)
    pick = row - seg * BASE
    one = jnp.where(row[:BASE] == lane[:BASE] % BASE, 1.0, 0.0).astype(F32)
    r = [one] * count
    for i in range(BASE - 1):
        spread = mm(packed, jnp.where(pick == i, 1.0, 0.0).astype(BF16))
        top = (i + 1) // 8 * 8
        for k in range(count):
            x = r[k][i : i + 1] * recip[k][i : i + 1]
            tail = r[k][top:] - spread[k * BASE + top : (k + 1) * BASE] * x
            r[k] = jnp.concatenate([r[k][:top], tail], axis=0) if top else tail
    out = []
    for k in range(count):
        x = r[k] * recip[k]
        out.append(jnp.where(row // BASE == seg, jnp.concatenate([x] * (BLK // BASE), axis=0), 0.0))
    size = BASE
    while size < BLK:
        off = (row // size > lane // size) & (row // (2 * size) == lane // (2 * size))
        half = [dot_exact_right(x, jnp.where(off, blk, 0.0).astype(BF16)) for x, blk in zip(out, low)]
        out = [x - dot3(h, x) for x, h in zip(out, half)]
        size *= 2
    return out


def join_blocks(first, second, low):
    off = -dot3(second, dot_exact_left(low, first))
    top = jnp.concatenate([first, jnp.zeros_like(first)], axis=1)
    return jnp.concatenate([top, jnp.concatenate([off, second], axis=1)], axis=0)


def substitute(inverse, upper, right):
    xs = []
    for j, inv in enumerate(inverse):
        r = right[:, j * BIG : (j + 1) * BIG]
        if j:
            r = r - dot_exact_right(jnp.concatenate(xs, axis=1), upper(j * BIG, j))
        xs.append(dot3(r, inv, trans=True))
    return jnp.concatenate(xs, axis=1)


def scaled(x):
    largest = jnp.max(jnp.abs(x), axis=1, keepdims=True)
    power = jnp.clip(jnp.ceil(jnp.log2(largest)), -100.0, 127.0)
    return jnp.concatenate([x * jnp.exp2(SPAN - power), jnp.broadcast_to(power, (x.shape[0], BLK))], axis=1)


def invert_panel(panel, pivot):
    blocks = pivot.shape[1] // BLK
    at = [slice(i * BLK, (i + 1) * BLK) for i in range(blocks)]
    small = invert_blocks([panel[s, s].astype(F32).T for s in at], [pivot[:, s] for s in at])
    return [
        join_blocks(small[i], small[i + 1], panel[at[i], at[i + 1]].astype(F32).T.astype(BF16))
        for i in range(0, blocks, 2)
    ]


def scaled_rows(x):
    largest = jnp.max(jnp.abs(x), axis=0, keepdims=True)
    power = jnp.clip(jnp.ceil(jnp.log2(largest)), -100.0, 127.0)
    return jnp.concatenate([x * jnp.exp2(SPAN - power), jnp.broadcast_to(power, (8, x.shape[1]))], axis=0)


def assemble(panel_ref, own_ref, other_ref):
    core = lax.axis_index("c")
    groups, count, w, _ = own_ref.shape
    for k in range(count):
        into = panel_ref.at[k]
        for g in range(groups):
            into[pl.ds(pl.multiple_of((2 * g + core) * w, w), w)] = own_ref[g, k]
            into[pl.ds(pl.multiple_of((2 * g + 1 - core) * w, w), w)] = other_ref[g, k]


def first_kernel(own_ref, other_ref, pivot_ref, right_ref, x_ref, sent_ref, hop_ref, panel_ref):
    me = lax.axis_index(ROW)

    @pl.when(me < panel_ref.shape[0])
    def _():
        assemble(panel_ref, own_ref, other_ref)

    @pl.when(me == 0)
    def _():
        inverse = invert_panel(panel_ref.at[0], pivot_ref[0:1])
        x = substitute(inverse, lambda n, j: panel_ref[0, :n, j * BIG : (j + 1) * BIG], right_ref[...].T)
        x_ref[...] = x
        sent_ref[...] = scaled(x)
        hop_ref[...] = scaled_rows(x)


def invert_kernel(panel_ref, pivot_ref, right_ref, inv_ref, turned_ref):
    @pl.when(lax.axis_index(ROW) == 1)
    def _():
        turned_ref[...] = right_ref[...].T
        for i, inv in enumerate(invert_panel(panel_ref.at[1], pivot_ref[1:2])):
            inv_ref[i] = inv


def second_kernel(got_ref, panel_ref, inv_ref, turned_ref, x_ref, sent_ref, out_ref, out_sent_ref):
    me = lax.axis_index(ROW)

    @pl.when(me == 0)
    def _():
        out_ref[...] = x_ref[...]
        out_sent_ref[...] = sent_ref[...]

    @pl.when(me == 1)
    def _():
        inverse = [inv_ref[i] for i in range(inv_ref.shape[0])]
        x = got_ref[:-8] * jnp.exp2(got_ref[-8:-7] - SPAN)
        right = turned_ref[...] - dot_exact_right(x, panel_ref[0])
        x = substitute(inverse, lambda n, j: panel_ref[1, :n, j * BIG : (j + 1) * BIG], right)
        out_ref[...] = x
        out_sent_ref[...] = scaled(x)


def last_kernel(own_ref, other_ref, pieces_ref, x_ref, right_ref, out_ref, panel_ref):
    count, width, _ = panel_ref.shape
    columns = x_ref.shape[0]
    me = lax.axis_index(ROW)

    @pl.when(me < count)
    def _():
        out_ref[...] = x_ref[...].T

    @pl.when(me >= count)
    def _():
        assemble(panel_ref, own_ref, other_ref)
        got = pieces_ref[...].reshape(columns, count * width + BLK)
        update = 0.0
        for k in range(count):
            at = count * width + k * BLK // count
            x = got[:, k * width : (k + 1) * width] * jnp.exp2(got[:, at : at + 1] - SPAN)
            update = update + dot_exact_right(x, panel_ref[k])
        out_ref[...] = right_ref[...] - update.T


def on_chip(kernel, out_shape, n_in, scratch=()):
    vmem = pl.BlockSpec(memory_space=pltpu.VMEM)
    return pl.pallas_call(
        kernel,
        out_shape=out_shape,
        in_specs=[vmem] * n_in,
        out_specs=jax.tree.map(lambda _: vmem, out_shape),
        scratch_shapes=list(scratch),
        compiler_params=pltpu.CompilerParams(vmem_limit_bytes=24 * 1024 * 1024),
    )


def same_to_all(piece, axes):
    count = lax.axis_size(axes)
    return lax.all_to_all(jnp.broadcast_to(piece[None], (count, *piece.shape)), axes, 0, 0, tiled=True)


def whole(factor, pivots, right):
    count, rows, w = factor.shape
    width = pivots.shape[1]
    columns = right.shape[1]
    n = lax.axis_size(ROW)

    piece = jnp.swapaxes(factor, 1, 2)
    own = same_to_all(same_to_all(piece, "zl"), "x").reshape(-1, count, w, rows)
    swap = [[(2 * r + c, 2 * r + 1 - c) for r in group for c in (0, 1)] for group in (range(count), range(count, n))]
    other = lax.ppermute(own, ROW + ("c",), swap[0])
    other_late = lax.ppermute(own, ROW + ("c",), swap[1])

    solved = (jax.ShapeDtypeStruct((columns, width), F32), jax.ShapeDtypeStruct((columns, width + BLK), F32))
    all_cols = (jax.ShapeDtypeStruct((count, width, rows), BF16),)
    kept = (jax.ShapeDtypeStruct((width // BIG, BIG, BIG), F32), jax.ShapeDtypeStruct((columns, width), F32))
    hop = (jax.ShapeDtypeStruct((columns + 8, width), F32),)
    x, sent, hop, panel = on_chip(first_kernel, solved + hop + all_cols, 4)(own, other, pivots, right)
    got = lax.ppermute(hop.astype(jnp.float16), ROW, [(0, 1)])
    inverse, turned = on_chip(invert_kernel, kept, 3)(panel, pivots, right)
    x, sent = on_chip(second_kernel, solved, 6)(got.astype(F32), panel, inverse, turned, x, sent)
    sent = sent.astype(jnp.float16).reshape(n, columns // n, width + BLK)
    mine = lax.all_to_all(sent, ROW, 0, 0, tiled=True)[:count]
    share = BLK // count
    power = [mine[k, :, width + k * share : width + (k + 1) * share] for k in range(count)]
    mine = jnp.concatenate([mine[k, :, :width] for k in range(count)] + power, axis=1)
    pieces = same_to_all(mine, ROW).astype(F32)
    scratch = [pltpu.VMEM((count, width, rows), BF16)]
    out = jax.ShapeDtypeStruct((rows, columns), F32)
    return on_chip(last_kernel, out, 5, scratch)(own, other_late, pieces, x, right)


def solution(mesh):
    ids = mesh.devices
    shape = (2, ids.shape[0] // 4, 2, ids.shape[1] // 8, 4, 2)
    split = Mesh(ids.reshape(shape), ROW + RHS)
    return jax.shard_map(
        whole,
        mesh=split,
        in_specs=(P(None, ROW, RHS), P(), P(ROW, RHS)),
        out_specs=P(ROW, RHS),
        check_vma=False,
    )
```

```python
import jax
import jax.numpy as jnp
from jax import lax
from jax.experimental import pallas as pl
from jax.experimental.pallas import tpu as pltpu
from jax.sharding import Mesh
from jax.sharding import PartitionSpec as P


ROW = ("zh", "yh", "yl")
RHS = ("x", "zl", "c")
F32, BF16 = jnp.float32, jnp.bfloat16
BASE, BLK, BIG = 32, 128, 256
SPAN = 14.0


def split2(v):
    hi = v.astype(BF16)
    lo = (v - hi.astype(F32)).astype(BF16)
    return hi, lo


def mm(a, b, trans=False):
    return lax.dot_general(a, b, (((1,), (1 if trans else 0,)), ((), ())), preferred_element_type=F32)


def dot_exact_left(a, v):
    n = v.shape[1]
    both = mm(a, jnp.concatenate(split2(v), axis=1))
    return both[:, :n] + both[:, n:]


def dot_exact_right(v, b):
    m = v.shape[0]
    both = mm(jnp.concatenate(split2(v), axis=0), b)
    return both[:m] + both[m:]


def dot3(a, b, trans=False):
    m = a.shape[0]
    ah, al = split2(a)
    bh, bl = split2(b)
    both = mm(jnp.concatenate([ah, al], axis=0), bh, trans)
    return both[:m] + (both[m:] + mm(ah, bl, trans))


def iota(shape, dim):
    return lax.broadcasted_iota(jnp.int32, shape, dim)


def spread_recip(pivot, row, seg):
    lane = iota((BASE, BLK), 1)
    left = jnp.where(lane % BASE == iota((BASE, BLK), 0), pivot, 0.0)
    same = jnp.where(row // BASE == seg, 1.0, 0.0).astype(BF16)
    a, rest = split2(left)
    b = rest
    c = (left - a.astype(F32) - b.astype(F32)).astype(BF16)
    got = mm(jnp.concatenate([a, b, c], axis=0), same)
    return 1.0 / (got[:BASE] + got[BASE : 2 * BASE] + got[2 * BASE :])


def invert_blocks(low, pivot):
    count = len(low)
    row, lane = iota((BLK, BLK), 0), iota((BLK, BLK), 1)
    seg = lane // BASE
    recip = [spread_recip(p, row, seg) for p in pivot]
    packed = []
    for blk in low:
        strict = jnp.where(row > lane, blk, 0.0)
        part = strict[:BASE]
        for s in range(1, BLK // BASE):
            part = jnp.where(seg[:BASE] == s, strict[s * BASE : (s + 1) * BASE], part)
        packed.append(part)
    packed = jnp.concatenate(packed, axis=0).astype(BF16)
    pick = row - seg * BASE
    one = jnp.where(row[:BASE] == lane[:BASE] % BASE, 1.0, 0.0).astype(F32)
    r = [one] * count
    for i in range(BASE - 1):
        spread = mm(packed, jnp.where(pick == i, 1.0, 0.0).astype(BF16))
        top = (i + 1) // 8 * 8
        for k in range(count):
            x = r[k][i : i + 1] * recip[k][i : i + 1]
            tail = r[k][top:] - spread[k * BASE + top : (k + 1) * BASE] * x
            r[k] = jnp.concatenate([r[k][:top], tail], axis=0) if top else tail
    out = []
    for k in range(count):
        x = r[k] * recip[k]
        out.append(jnp.where(row // BASE == seg, jnp.concatenate([x] * (BLK // BASE), axis=0), 0.0))
    size = BASE
    while size < BLK:
        off = (row // size > lane // size) & (row // (2 * size) == lane // (2 * size))
        half = [dot_exact_right(x, jnp.where(off, blk, 0.0).astype(BF16)) for x, blk in zip(out, low)]
        out = [x - dot3(h, x) for x, h in zip(out, half)]
        size *= 2
    return out


def join_blocks(first, second, low):
    off = -dot3(second, dot_exact_left(low, first))
    top = jnp.concatenate([first, jnp.zeros_like(first)], axis=1)
    return jnp.concatenate([top, jnp.concatenate([off, second], axis=1)], axis=0)


def substitute(inverse, upper, right):
    xs = []
    for j, inv in enumerate(inverse):
        r = right[:, j * BIG : (j + 1) * BIG]
        if j:
            r = r - dot_exact_right(jnp.concatenate(xs, axis=1), upper(j * BIG, j))
        xs.append(dot3(r, inv, trans=True))
    return jnp.concatenate(xs, axis=1)


def power_of(largest):
    return jnp.clip(jnp.ceil(jnp.log2(largest)), -100.0, 127.0)


def scaled(x):
    blocks = x.shape[1] // BLK
    lane = iota((x.shape[0], BLK), 1) // (BLK // 2 // blocks) % blocks
    out, powers = [], jnp.zeros((x.shape[0], BLK), F32)
    for j in range(blocks):
        part = x[:, j * BLK : (j + 1) * BLK]
        power = power_of(jnp.max(jnp.abs(part), axis=1, keepdims=True))
        out.append(part * jnp.exp2(SPAN - power))
        powers = jnp.where(lane == j, power, powers)
    return jnp.concatenate(out + [powers], axis=1)


def invert_panel(panel, pivot):
    blocks = pivot.shape[1] // BLK
    at = [slice(i * BLK, (i + 1) * BLK) for i in range(blocks)]
    small = invert_blocks([panel[s, s].astype(F32).T for s in at], [pivot[:, s] for s in at])
    return [
        join_blocks(small[i], small[i + 1], panel[at[i], at[i + 1]].astype(F32).T.astype(BF16))
        for i in range(0, blocks, 2)
    ]


def scaled_rows(x):
    power = power_of(jnp.max(jnp.abs(x), axis=0, keepdims=True))
    return jnp.concatenate([x * jnp.exp2(SPAN - power), jnp.broadcast_to(power, (8, x.shape[1]))], axis=0)


def assemble(panel_ref, own_ref, other_ref):
    core = lax.axis_index("c")
    groups, count, w, _ = own_ref.shape
    for k in range(count):
        into = panel_ref.at[k]
        for g in range(groups):
            into[pl.ds(pl.multiple_of((2 * g + core) * w, w), w)] = own_ref[g, k]
            into[pl.ds(pl.multiple_of((2 * g + 1 - core) * w, w), w)] = other_ref[g, k]


def first_kernel(own_ref, other_ref, pivot_ref, right_ref, x_ref, sent_ref, hop_ref, panel_ref):
    me = lax.axis_index(ROW)

    @pl.when(me < panel_ref.shape[0])
    def _():
        assemble(panel_ref, own_ref, other_ref)

    @pl.when(me == 0)
    def _():
        inverse = invert_panel(panel_ref.at[0], pivot_ref[0:1])
        x = substitute(inverse, lambda n, j: panel_ref[0, :n, j * BIG : (j + 1) * BIG], right_ref[...].T)
        x_ref[...] = x
        sent_ref[...] = scaled(x)
        hop_ref[...] = scaled_rows(x)


def invert_kernel(panel_ref, pivot_ref, right_ref, inv_ref, turned_ref):
    @pl.when(lax.axis_index(ROW) == 1)
    def _():
        turned_ref[...] = right_ref[...].T
        for i, inv in enumerate(invert_panel(panel_ref.at[1], pivot_ref[1:2])):
            inv_ref[i] = inv


def second_kernel(got_ref, panel_ref, inv_ref, turned_ref, x_ref, sent_ref, out_ref, out_sent_ref):
    me = lax.axis_index(ROW)

    @pl.when(me == 0)
    def _():
        out_ref[...] = x_ref[...]
        out_sent_ref[...] = sent_ref[...]

    @pl.when(me == 1)
    def _():
        inverse = [inv_ref[i] for i in range(inv_ref.shape[0])]
        x = got_ref[:-8] * jnp.exp2(got_ref[-8:-7] - SPAN)
        right = turned_ref[...] - dot_exact_right(x, panel_ref[0])
        x = substitute(inverse, lambda n, j: panel_ref[1, :n, j * BIG : (j + 1) * BIG], right)
        out_ref[...] = x
        out_sent_ref[...] = scaled(x)


def last_kernel(own_ref, other_ref, pieces_ref, x_ref, right_ref, out_ref, panel_ref):
    count, width, _ = panel_ref.shape
    columns = x_ref.shape[0]
    me = lax.axis_index(ROW)

    @pl.when(me < count)
    def _():
        out_ref[...] = x_ref[...].T

    @pl.when(me >= count)
    def _():
        assemble(panel_ref, own_ref, other_ref)
        got = pieces_ref[...].reshape(columns, count * width + BLK)
        update = 0.0
        for k in range(count):
            parts = []
            for j in range(width // BLK):
                at = k * width + j * BLK
                lane = count * width + at * BLK // (count * width)
                power = got[:, lane : lane + 1]
                parts.append(got[:, at : at + BLK] * jnp.exp2(power - SPAN))
            update = update + dot_exact_right(jnp.concatenate(parts, axis=1), panel_ref[k])
        out_ref[...] = right_ref[...] - update.T


def on_chip(kernel, out_shape, n_in, scratch=()):
    vmem = pl.BlockSpec(memory_space=pltpu.VMEM)
    return pl.pallas_call(
        kernel,
        out_shape=out_shape,
        in_specs=[vmem] * n_in,
        out_specs=jax.tree.map(lambda _: vmem, out_shape),
        scratch_shapes=list(scratch),
        compiler_params=pltpu.CompilerParams(vmem_limit_bytes=24 * 1024 * 1024),
    )


def same_to_all(piece, axes):
    count = lax.axis_size(axes)
    return lax.all_to_all(jnp.broadcast_to(piece[None], (count, *piece.shape)), axes, 0, 0, tiled=True)


def whole(factor, pivots, right):
    count, rows, w = factor.shape
    width = pivots.shape[1]
    columns = right.shape[1]
    n = lax.axis_size(ROW)

    piece = jnp.swapaxes(factor, 1, 2)
    own = same_to_all(same_to_all(piece, "zl"), "x").reshape(-1, count, w, rows)
    swap = [[(2 * r + c, 2 * r + 1 - c) for r in group for c in (0, 1)] for group in (range(count), range(count, n))]
    other = lax.ppermute(own, ROW + ("c",), swap[0])
    other_late = lax.ppermute(own, ROW + ("c",), swap[1])

    solved = (jax.ShapeDtypeStruct((columns, width), F32), jax.ShapeDtypeStruct((columns, width + BLK), F32))
    all_cols = (jax.ShapeDtypeStruct((count, width, rows), BF16),)
    kept = (jax.ShapeDtypeStruct((width // BIG, BIG, BIG), F32), jax.ShapeDtypeStruct((columns, width), F32))
    hop = (jax.ShapeDtypeStruct((columns + 8, width), F32),)
    x, sent, hop, panel = on_chip(first_kernel, solved + hop + all_cols, 4)(own, other, pivots, right)
    got = lax.ppermute(hop.astype(jnp.float16), ROW, [(0, 1)])
    inverse, turned = on_chip(invert_kernel, kept, 3)(panel, pivots, right)
    x, sent = on_chip(second_kernel, solved, 6)(got.astype(F32), panel, inverse, turned, x, sent)
    sent = sent.astype(jnp.float16).reshape(n, columns // n, width + BLK)
    mine = lax.all_to_all(sent, ROW, 0, 0, tiled=True)[:count]
    share = BLK // count
    power = [mine[k, :, width + k * share : width + (k + 1) * share] for k in range(count)]
    mine = jnp.concatenate([mine[k, :, :width] for k in range(count)] + power, axis=1)
    pieces = same_to_all(mine, ROW).astype(F32)
    scratch = [pltpu.VMEM((count, width, rows), BF16)]
    out = jax.ShapeDtypeStruct((rows, columns), F32)
    return on_chip(last_kernel, out, 5, scratch)(own, other_late, pieces, x, right)


def solution(mesh):
    ids = mesh.devices
    shape = (2, ids.shape[0] // 4, 2, ids.shape[1] // 8, 4, 2)
    split = Mesh(ids.reshape(shape), ROW + RHS)
    return jax.shard_map(
        whole,
        mesh=split,
        in_specs=(P(None, ROW, RHS), P(), P(ROW, RHS)),
        out_specs=P(ROW, RHS),
        check_vma=False,
    )
```

```python
import jax
import jax.numpy as jnp
from jax import lax
from jax.experimental import pallas as pl
from jax.experimental.pallas import tpu as pltpu
from jax.sharding import Mesh
from jax.sharding import PartitionSpec as P


ROW = ("zh", "yh", "yl")
RHS = ("x", "zl", "c")
F32, BF16 = jnp.float32, jnp.bfloat16
BASE, BLK, BIG = 32, 128, 256
SPAN = 14.0


def split2(v):
    hi = v.astype(BF16)
    lo = (v - hi.astype(F32)).astype(BF16)
    return hi, lo


def mm(a, b, trans=False):
    return lax.dot_general(a, b, (((1,), (1 if trans else 0,)), ((), ())), preferred_element_type=F32)


def dot_exact_left(a, v):
    n = v.shape[1]
    both = mm(a, jnp.concatenate(split2(v), axis=1))
    return both[:, :n] + both[:, n:]


def dot_exact_right(v, b):
    m = v.shape[0]
    both = mm(jnp.concatenate(split2(v), axis=0), b)
    return both[:m] + both[m:]


def dot3(a, b, trans=False):
    m = a.shape[0]
    ah, al = split2(a)
    bh, bl = split2(b)
    both = mm(jnp.concatenate([ah, al], axis=0), bh, trans)
    return both[:m] + (both[m:] + mm(ah, bl, trans))


def iota(shape, dim):
    return lax.broadcasted_iota(jnp.int32, shape, dim)


def spread_recip(pivot, row, seg):
    lane = iota((BASE, BLK), 1)
    left = jnp.where(lane % BASE == iota((BASE, BLK), 0), pivot, 0.0)
    same = jnp.where(row // BASE == seg, 1.0, 0.0).astype(BF16)
    a, rest = split2(left)
    b = rest
    c = (left - a.astype(F32) - b.astype(F32)).astype(BF16)
    got = mm(jnp.concatenate([a, b, c], axis=0), same)
    return 1.0 / (got[:BASE] + got[BASE : 2 * BASE] + got[2 * BASE :])


def invert_blocks(low, pivot):
    count = len(low)
    row, lane = iota((BLK, BLK), 0), iota((BLK, BLK), 1)
    seg = lane // BASE
    recip = [spread_recip(p, row, seg) for p in pivot]
    packed = []
    for blk in low:
        strict = jnp.where(row > lane, blk, 0.0)
        part = strict[:BASE]
        for s in range(1, BLK // BASE):
            part = jnp.where(seg[:BASE] == s, strict[s * BASE : (s + 1) * BASE], part)
        packed.append(part)
    packed = jnp.concatenate(packed, axis=0).astype(BF16)
    pick = row - seg * BASE
    one = jnp.where(row[:BASE] == lane[:BASE] % BASE, 1.0, 0.0).astype(F32)
    r = [one] * count
    for i in range(BASE - 1):
        if i % 2 == 0:
            two = jnp.concatenate([jnp.where(pick == i + j, 1.0, 0.0) for j in range(2)], axis=1).astype(BF16)
            two = mm(packed, two)
        spread = two[:, i % 2 * BLK : (i % 2 + 1) * BLK]
        top = (i + 1) // 8 * 8
        for k in range(count):
            x = r[k][i : i + 1] * recip[k][i : i + 1]
            tail = r[k][top:] - spread[k * BASE + top : (k + 1) * BASE] * x
            r[k] = jnp.concatenate([r[k][:top], tail], axis=0) if top else tail
    out = []
    for k in range(count):
        x = r[k] * recip[k]
        out.append(jnp.where(row // BASE == seg, jnp.concatenate([x] * (BLK // BASE), axis=0), 0.0))
    size = BASE
    while size < BLK:
        off = (row // size > lane // size) & (row // (2 * size) == lane // (2 * size))
        half = [dot_exact_right(x, jnp.where(off, blk, 0.0).astype(BF16)) for x, blk in zip(out, low)]
        out = [x - dot3(h, x) for x, h in zip(out, half)]
        size *= 2
    return out


def join_blocks(first, second, low):
    off = -dot3(second, dot_exact_left(low, first))
    top = jnp.concatenate([first, jnp.zeros_like(first)], axis=1)
    return jnp.concatenate([top, jnp.concatenate([off, second], axis=1)], axis=0)


def substitute(inverse, upper, right):
    xs = []
    for j, inv in enumerate(inverse):
        r = right[:, j * BIG : (j + 1) * BIG]
        if j:
            r = r - dot_exact_right(jnp.concatenate(xs, axis=1), upper(j * BIG, j))
        xs.append(dot3(r, inv, trans=True))
    return jnp.concatenate(xs, axis=1)


def power_of(largest):
    return jnp.clip(jnp.ceil(jnp.log2(largest)), -100.0, 127.0)


def scaled(x):
    blocks = x.shape[1] // BLK
    lane = iota((x.shape[0], BLK), 1) // (BLK // 2 // blocks) % blocks
    out, powers = [], jnp.zeros((x.shape[0], BLK), F32)
    for j in range(blocks):
        part = x[:, j * BLK : (j + 1) * BLK]
        power = power_of(jnp.max(jnp.abs(part), axis=1, keepdims=True))
        out.append(part * jnp.exp2(SPAN - power))
        powers = jnp.where(lane == j, power, powers)
    return jnp.concatenate(out + [powers], axis=1)


def invert_panel(panel, pivot):
    blocks = pivot.shape[1] // BLK
    at = [slice(i * BLK, (i + 1) * BLK) for i in range(blocks)]
    small = invert_blocks([panel[s, s].astype(F32).T for s in at], [pivot[:, s] for s in at])
    return [
        join_blocks(small[i], small[i + 1], panel[at[i], at[i + 1]].astype(F32).T.astype(BF16))
        for i in range(0, blocks, 2)
    ]


def scaled_rows(x):
    power = power_of(jnp.max(jnp.abs(x), axis=0, keepdims=True))
    return jnp.concatenate([x * jnp.exp2(SPAN - power), jnp.broadcast_to(power, (8, x.shape[1]))], axis=0)


def assemble(panel_ref, own_ref, other_ref):
    core = lax.axis_index("c")
    groups, count, w, _ = own_ref.shape
    for k in range(count):
        into = panel_ref.at[k]
        for g in range(groups):
            into[pl.ds(pl.multiple_of((2 * g + core) * w, w), w)] = own_ref[g, k]
            into[pl.ds(pl.multiple_of((2 * g + 1 - core) * w, w), w)] = other_ref[g, k]


def first_kernel(cols_ref, pivot_ref, right_ref, x_ref, sent_ref, hop_ref, panel_ref):
    cores, groups, w, _ = cols_ref.shape
    for g in range(groups):
        for c in range(cores):
            at = (cores * g + c) * w
            panel_ref[at : at + w] = cols_ref[c, g]

    @pl.when(lax.axis_index(ROW) == 0)
    def _():
        inverse = invert_panel(panel_ref, pivot_ref[0:1])
        x = substitute(inverse, lambda n, j: panel_ref[:n, j * BIG : (j + 1) * BIG], right_ref[...].T)
        x_ref[...] = x
        sent_ref[...] = scaled(x)
        hop_ref[...] = scaled_rows(x)


def invert_kernel(panel_ref, pivot_ref, right_ref, inv_ref, turned_ref):
    @pl.when(lax.axis_index(ROW) == 1)
    def _():
        turned_ref[...] = right_ref[...].T
        for i, inv in enumerate(invert_panel(panel_ref, pivot_ref[1:2])):
            inv_ref[i] = inv


def second_kernel(
    got_ref, own_ref, other_ref, panel_ref, inv_ref, turned_ref, x_ref, sent_ref, out_ref, out_sent_ref, low_ref
):
    me = lax.axis_index(ROW)

    @pl.when(me == 0)
    def _():
        out_ref[...] = x_ref[...]
        out_sent_ref[...] = sent_ref[...]

    @pl.when(me == 1)
    def _():
        inverse = [inv_ref[i] for i in range(inv_ref.shape[0])]
        x = got_ref[:-8] * jnp.exp2(got_ref[-8:-7] - SPAN)
        assemble(low_ref, own_ref, other_ref)
        right = turned_ref[...] - dot_exact_right(x, low_ref[0])
        x = substitute(inverse, lambda n, j: panel_ref[:n, j * BIG : (j + 1) * BIG], right)
        out_ref[...] = x
        out_sent_ref[...] = scaled(x)


def last_kernel(own_ref, other_ref, pieces_ref, x_ref, right_ref, out_ref, panel_ref):
    count, width, _ = panel_ref.shape
    columns = x_ref.shape[0]
    me = lax.axis_index(ROW)

    @pl.when(me < count)
    def _():
        out_ref[...] = x_ref[...].T

    @pl.when(me >= count)
    def _():
        assemble(panel_ref, own_ref, other_ref)
        got = pieces_ref[...].reshape(columns, count * width + BLK)
        update = 0.0
        for k in range(count):
            parts = []
            for j in range(width // BLK):
                at = k * width + j * BLK
                lane = count * width + at * BLK // (count * width)
                power = got[:, lane : lane + 1]
                parts.append(got[:, at : at + BLK] * jnp.exp2(power - SPAN))
            update = update + dot_exact_right(jnp.concatenate(parts, axis=1), panel_ref[k])
        out_ref[...] = right_ref[...] - update.T


def on_chip(kernel, out_shape, n_in, scratch=()):
    vmem = pl.BlockSpec(memory_space=pltpu.VMEM)
    return pl.pallas_call(
        kernel,
        out_shape=out_shape,
        in_specs=[vmem] * n_in,
        out_specs=jax.tree.map(lambda _: vmem, out_shape),
        scratch_shapes=list(scratch),
        compiler_params=pltpu.CompilerParams(vmem_limit_bytes=24 * 1024 * 1024),
    )


def same_to_all(piece, axes):
    count = lax.axis_size(axes)
    return lax.all_to_all(jnp.broadcast_to(piece[None], (count, *piece.shape)), axes, 0, 0, tiled=True)


def whole(factor, pivots, right):
    count, rows, w = factor.shape
    width = pivots.shape[1]
    columns = right.shape[1]
    n = lax.axis_size(ROW)

    piece = jnp.swapaxes(factor, 1, 2)
    near = same_to_all(piece, "zl")
    own = same_to_all(near, "x").reshape(-1, count, w, rows)
    swap = [(2 * r + c, 2 * r + 1 - c) for r in range(count, n) for c in (0, 1)]
    other_late = lax.ppermute(own, ROW + ("c",), swap)
    solved = (jax.ShapeDtypeStruct((columns, width), F32), jax.ShapeDtypeStruct((columns, width + BLK), F32))

    def solve(own, pivots, right):
        me = lax.axis_index(ROW)
        mine = lax.dynamic_index_in_dim(own, me, 1, False)
        rest = lax.dynamic_slice_in_dim(own, 1 - me, 1, 1)
        both = lax.all_gather(mine, "c")
        other = jax.ShapeDtypeStruct((columns + 8, width), F32), jax.ShapeDtypeStruct((width, rows), BF16)
        kept = (jax.ShapeDtypeStruct((width // BIG, BIG, BIG), F32), jax.ShapeDtypeStruct((columns, width), F32))
        x, sent, hop, panel = on_chip(first_kernel, solved + other, 3)(both, pivots, right)
        got = lax.ppermute(hop.astype(jnp.float16), ROW, [(0, 1)])
        swap = [(2 * r + c, 2 * r + 1 - c) for r in range(count) for c in (0, 1)]
        low = lax.ppermute(rest, ROW + ("c",), swap)
        inverse, turned = on_chip(invert_kernel, kept, 3)(panel, pivots, right)
        scratch = [pltpu.VMEM((1, width, rows), BF16)]
        return on_chip(second_kernel, solved, 8, scratch)(
            got.astype(F32), rest, low, panel, inverse, turned, x, sent
        )

    def skip(own, pivots, right):
        return on_chip(lambda *refs: None, solved, 1)(right)

    x, sent = lax.cond(lax.axis_index(ROW) < count, solve, skip, own, pivots, right)
    sent = sent.astype(jnp.float16).reshape(n, columns // n, width + BLK)
    mine = lax.all_to_all(sent, ROW, 0, 0, tiled=True)[:count]
    share = BLK // count
    power = [mine[k, :, width + k * share : width + (k + 1) * share] for k in range(count)]
    mine = jnp.concatenate([mine[k, :, :width] for k in range(count)] + power, axis=1)
    pieces = same_to_all(mine, ROW).astype(F32)
    scratch = [pltpu.VMEM((count, width, rows), BF16)]
    out = jax.ShapeDtypeStruct((rows, columns), F32)
    return on_chip(last_kernel, out, 5, scratch)(own, other_late, pieces, x, right)


def solution(mesh):
    ids = mesh.devices
    shape = (2, ids.shape[0] // 4, 2, ids.shape[1] // 8, 4, 2)
    split = Mesh(ids.reshape(shape), ROW + RHS)
    return jax.shard_map(
        whole,
        mesh=split,
        in_specs=(P(None, ROW, RHS), P(), P(ROW, RHS)),
        out_specs=P(ROW, RHS),
        check_vma=False,
    )
```

```python
import jax
import jax.numpy as jnp
from jax import lax
from jax.experimental import pallas as pl
from jax.experimental.pallas import tpu as pltpu
from jax.sharding import Mesh
from jax.sharding import PartitionSpec as P


ROW = ("zh", "yh", "yl")
RHS = ("x", "zl", "c")
F32, BF16 = jnp.float32, jnp.bfloat16
BASE, BLK, BIG = 32, 128, 256
SPAN = 14.0


def split2(v):
    hi = v.astype(BF16)
    lo = (v - hi.astype(F32)).astype(BF16)
    return hi, lo


def mm(a, b, trans=False):
    return lax.dot_general(a, b, (((1,), (1 if trans else 0,)), ((), ())), preferred_element_type=F32)


def dot_exact_left(a, v):
    n = v.shape[1]
    both = mm(a, jnp.concatenate(split2(v), axis=1))
    return both[:, :n] + both[:, n:]


def dot_exact_right(v, b):
    m = v.shape[0]
    both = mm(jnp.concatenate(split2(v), axis=0), b)
    return both[:m] + both[m:]


def dot3(a, b, trans=False):
    m = a.shape[0]
    ah, al = split2(a)
    bh, bl = split2(b)
    both = mm(jnp.concatenate([ah, al], axis=0), bh, trans)
    return both[:m] + (both[m:] + mm(ah, bl, trans))


def iota(shape, dim):
    return lax.broadcasted_iota(jnp.int32, shape, dim)


def spread_recip(pivot, row, seg):
    lane = iota((BASE, BLK), 1)
    left = jnp.where(lane % BASE == iota((BASE, BLK), 0), pivot, 0.0)
    same = jnp.where(row // BASE == seg, 1.0, 0.0).astype(BF16)
    a, rest = split2(left)
    b = rest
    c = (left - a.astype(F32) - b.astype(F32)).astype(BF16)
    got = mm(jnp.concatenate([a, b, c], axis=0), same)
    return 1.0 / (got[:BASE] + got[BASE : 2 * BASE] + got[2 * BASE :])


def invert_blocks(low, pivot):
    count = len(low)
    row, lane = iota((BLK, BLK), 0), iota((BLK, BLK), 1)
    seg = lane // BASE
    recip = [spread_recip(p, row, seg) for p in pivot]
    packed = []
    for blk in low:
        strict = jnp.where(row > lane, blk, 0.0)
        part = strict[:BASE]
        for s in range(1, BLK // BASE):
            part = jnp.where(seg[:BASE] == s, strict[s * BASE : (s + 1) * BASE], part)
        packed.append(part)
    packed = jnp.concatenate(packed, axis=0).astype(BF16)
    pick = row - seg * BASE
    one = jnp.where(row[:BASE] == lane[:BASE] % BASE, 1.0, 0.0).astype(F32)
    r = [one] * count
    for i in range(BASE - 1):
        if i % 2 == 0:
            two = jnp.concatenate([jnp.where(pick == i + j, 1.0, 0.0) for j in range(2)], axis=1).astype(BF16)
            two = mm(packed, two)
        spread = two[:, i % 2 * BLK : (i % 2 + 1) * BLK]
        top = (i + 1) // 8 * 8
        for k in range(count):
            x = r[k][i : i + 1] * recip[k][i : i + 1]
            tail = r[k][top:] - spread[k * BASE + top : (k + 1) * BASE] * x
            r[k] = jnp.concatenate([r[k][:top], tail], axis=0) if top else tail
    out = []
    for k in range(count):
        x = r[k] * recip[k]
        out.append(jnp.where(row // BASE == seg, jnp.concatenate([x] * (BLK // BASE), axis=0), 0.0))
    size = BASE
    while size < BLK:
        off = (row // size > lane // size) & (row // (2 * size) == lane // (2 * size))
        half = [dot_exact_right(x, jnp.where(off, blk, 0.0).astype(BF16)) for x, blk in zip(out, low)]
        out = [x - dot3(h, x) for x, h in zip(out, half)]
        size *= 2
    return out


def join_blocks(first, second, low):
    off = -dot3(second, dot_exact_left(low, first))
    top = jnp.concatenate([first, jnp.zeros_like(first)], axis=1)
    return jnp.concatenate([top, jnp.concatenate([off, second], axis=1)], axis=0)


def substitute(inverse, upper, right):
    xs = []
    for j, inv in enumerate(inverse):
        r = right[:, j * BIG : (j + 1) * BIG]
        if j:
            r = r - dot_exact_right(jnp.concatenate(xs, axis=1), upper(j * BIG, j))
        xs.append(dot3(r, inv, trans=True))
    return jnp.concatenate(xs, axis=1)


def power_of(largest):
    return jnp.clip(jnp.ceil(jnp.log2(largest)), -100.0, 127.0)


def scaled(x):
    blocks = x.shape[1] // BLK
    lane = iota((x.shape[0], BLK), 1) // (BLK // 2 // blocks) % blocks
    out, powers = [], jnp.zeros((x.shape[0], BLK), F32)
    for j in range(blocks):
        part = x[:, j * BLK : (j + 1) * BLK]
        power = power_of(jnp.max(jnp.abs(part), axis=1, keepdims=True))
        out.append(part * jnp.exp2(SPAN - power))
        powers = jnp.where(lane == j, power, powers)
    return jnp.concatenate(out + [powers], axis=1)


def invert_panel(panel, pivot):
    blocks = pivot.shape[1] // BLK
    at = [slice(i * BLK, (i + 1) * BLK) for i in range(blocks)]
    small = invert_blocks([panel[s, s].astype(F32).T for s in at], [pivot[:, s] for s in at])
    return [
        join_blocks(small[i], small[i + 1], panel[at[i], at[i + 1]].astype(F32).T.astype(BF16))
        for i in range(0, blocks, 2)
    ]


def scaled_rows(x):
    power = power_of(jnp.max(jnp.abs(x), axis=0, keepdims=True))
    return jnp.concatenate([x * jnp.exp2(SPAN - power), jnp.broadcast_to(power, (8, x.shape[1]))], axis=0)


def assemble(panel_ref, own_ref, other_ref):
    core = lax.axis_index("c")
    groups, count, w, _ = own_ref.shape
    for k in range(count):
        into = panel_ref.at[k]
        for g in range(groups):
            into[pl.ds(pl.multiple_of((2 * g + core) * w, w), w)] = own_ref[g, k]
            into[pl.ds(pl.multiple_of((2 * g + 1 - core) * w, w), w)] = other_ref[g, k]


def first_kernel(cols_ref, pivot_ref, right_ref, x_ref, sent_ref, hop_ref, panel_ref):
    cores, groups, w, _ = cols_ref.shape
    for g in range(groups):
        for c in range(cores):
            at = (cores * g + c) * w
            panel_ref[at : at + w] = cols_ref[c, g]

    @pl.when(lax.axis_index(ROW) == 0)
    def _():
        inverse = invert_panel(panel_ref, pivot_ref[0:1])
        x = substitute(inverse, lambda n, j: panel_ref[:n, j * BIG : (j + 1) * BIG], right_ref[...].T)
        x_ref[...] = x
        sent_ref[...] = scaled(x)
        hop_ref[...] = scaled_rows(x)


def invert_kernel(panel_ref, pivot_ref, right_ref, inv_ref, turned_ref):
    @pl.when(lax.axis_index(ROW) == 1)
    def _():
        turned_ref[...] = right_ref[...].T
        for i, inv in enumerate(invert_panel(panel_ref, pivot_ref[1:2])):
            inv_ref[i] = inv


def second_kernel(
    got_ref, own_ref, other_ref, panel_ref, inv_ref, turned_ref, x_ref, sent_ref, out_ref, out_sent_ref, low_ref
):
    me = lax.axis_index(ROW)

    @pl.when(me == 0)
    def _():
        out_ref[...] = x_ref[...]
        out_sent_ref[...] = sent_ref[...]

    @pl.when(me == 1)
    def _():
        inverse = [inv_ref[i] for i in range(inv_ref.shape[0])]
        x = got_ref[:-8] * jnp.exp2(got_ref[-8:-7] - SPAN)
        assemble(low_ref, own_ref, other_ref)
        right = turned_ref[...] - dot_exact_right(x, low_ref[0])
        x = substitute(inverse, lambda n, j: panel_ref[:n, j * BIG : (j + 1) * BIG], right)
        out_ref[...] = x
        out_sent_ref[...] = scaled(x)


def last_kernel(own_ref, other_ref, pieces_ref, x_ref, right_ref, out_ref, panel_ref, done_ref, sems):
    count, width, rows = panel_ref.shape
    columns = x_ref.shape[0]
    me = lax.axis_index(ROW)
    halves = [slice(i * BIG, (i + 1) * BIG) for i in range(rows // BIG)]
    copies = [pltpu.make_async_copy(done_ref.at[h], out_ref.at[h], sems.at[i]) for i, h in enumerate(halves)]

    @pl.when(me < count)
    def _():
        for h, copy in zip(halves, copies):
            done_ref[h] = x_ref[:, h].T
            copy.start()

    @pl.when(me >= count)
    def _():
        assemble(panel_ref, own_ref, other_ref)
        got = pieces_ref[...].reshape(columns, count * width + BLK)
        parts = []
        for k in range(count):
            scaled_back = []
            for j in range(width // BLK):
                at = k * width + j * BLK
                lane = count * width + at * BLK // (count * width)
                scaled_back.append(got[:, at : at + BLK] * jnp.exp2(got[:, lane : lane + 1] - SPAN))
            parts.append(jnp.concatenate(split2(jnp.concatenate(scaled_back, axis=1)), axis=0))
        for h, copy in zip(halves, copies):
            both = sum(mm(parts[k], panel_ref[k, :, h]) for k in range(count))
            done_ref[h] = right_ref[h] - (both[:columns] + both[columns:]).T
            copy.start()

    for copy in copies:
        copy.wait()


def on_chip(kernel, out_shape, n_in, scratch=()):
    vmem = pl.BlockSpec(memory_space=pltpu.VMEM)
    return pl.pallas_call(
        kernel,
        out_shape=out_shape,
        in_specs=[vmem] * n_in,
        out_specs=jax.tree.map(lambda _: vmem, out_shape),
        scratch_shapes=list(scratch),
        compiler_params=pltpu.CompilerParams(vmem_limit_bytes=24 * 1024 * 1024),
    )


def same_to_all(piece, axes):
    count = lax.axis_size(axes)
    return lax.all_to_all(jnp.broadcast_to(piece[None], (count, *piece.shape)), axes, 0, 0, tiled=True)


def whole(factor, pivots, right):
    count, rows, w = factor.shape
    width = pivots.shape[1]
    columns = right.shape[1]
    n = lax.axis_size(ROW)

    piece = jnp.swapaxes(factor, 1, 2)
    near = same_to_all(piece, "zl")
    own = same_to_all(near, "x").reshape(-1, count, w, rows)
    swap = [(2 * r + c, 2 * r + 1 - c) for r in range(count, n) for c in (0, 1)]
    other_late = lax.ppermute(own, ROW + ("c",), swap)
    solved = (jax.ShapeDtypeStruct((columns, width), F32), jax.ShapeDtypeStruct((columns, width + BLK), F32))

    def solve(own, pivots, right):
        me = lax.axis_index(ROW)
        mine = lax.dynamic_index_in_dim(own, me, 1, False)
        rest = lax.dynamic_slice_in_dim(own, 1 - me, 1, 1)
        both = lax.all_gather(mine, "c")
        other = jax.ShapeDtypeStruct((columns + 8, width), F32), jax.ShapeDtypeStruct((width, rows), BF16)
        kept = (jax.ShapeDtypeStruct((width // BIG, BIG, BIG), F32), jax.ShapeDtypeStruct((columns, width), F32))
        x, sent, hop, panel = on_chip(first_kernel, solved + other, 3)(both, pivots, right)
        got = lax.ppermute(hop.astype(jnp.float16), ROW, [(0, 1)])
        swap = [(2 * r + c, 2 * r + 1 - c) for r in range(count) for c in (0, 1)]
        low = lax.ppermute(rest, ROW + ("c",), swap)
        inverse, turned = on_chip(invert_kernel, kept, 3)(panel, pivots, right)
        scratch = [pltpu.VMEM((1, width, rows), BF16)]
        return on_chip(second_kernel, solved, 8, scratch)(
            got.astype(F32), rest, low, panel, inverse, turned, x, sent
        )

    def skip(own, pivots, right):
        return on_chip(lambda *refs: None, solved, 1)(right)

    x, sent = lax.cond(lax.axis_index(ROW) < count, solve, skip, own, pivots, right)
    sent = sent.astype(jnp.float16).reshape(n, columns // n, width + BLK)
    mine = lax.all_to_all(sent, ROW, 0, 0, tiled=True)[:count]
    share = BLK // count
    power = [mine[k, :, width + k * share : width + (k + 1) * share] for k in range(count)]
    mine = jnp.concatenate([mine[k, :, :width] for k in range(count)] + power, axis=1)
    pieces = same_to_all(mine, ROW).astype(F32)
    scratch = [pltpu.VMEM((count, width, rows), BF16)]
    out = jax.ShapeDtypeStruct((rows, columns), F32)
    vmem = pl.BlockSpec(memory_space=pltpu.VMEM)
    return pl.pallas_call(
        last_kernel,
        out_shape=out,
        in_specs=[vmem] * 5,
        out_specs=pl.BlockSpec(memory_space=pl.ANY),
        scratch_shapes=[*scratch, pltpu.VMEM((rows, columns), F32), pltpu.SemaphoreType.DMA((rows // BIG,))],
        compiler_params=pltpu.CompilerParams(vmem_limit_bytes=24 * 1024 * 1024),
    )(own, other_late, pieces, x, right)


def solution(mesh):
    ids = mesh.devices
    shape = (2, ids.shape[0] // 4, 2, ids.shape[1] // 8, 4, 2)
    split = Mesh(ids.reshape(shape), ROW + RHS)
    return jax.shard_map(
        whole,
        mesh=split,
        in_specs=(P(None, ROW, RHS), P(), P(ROW, RHS)),
        out_specs=P(ROW, RHS),
        check_vma=False,
    )
```

```python
import jax
import jax.numpy as jnp
from jax import lax
from jax.experimental import pallas as pl
from jax.experimental.pallas import tpu as pltpu
from jax.sharding import Mesh
from jax.sharding import PartitionSpec as P


ROW = ("zh", "yh", "yl")
RHS = ("x", "zl", "c")
F32, BF16 = jnp.float32, jnp.bfloat16
BASE, BLK, BIG = 32, 128, 256
SPAN = 14.0


def split2(v):
    hi = v.astype(BF16)
    lo = (v - hi.astype(F32)).astype(BF16)
    return hi, lo


def mm(a, b, trans=False):
    return lax.dot_general(a, b, (((1,), (1 if trans else 0,)), ((), ())), preferred_element_type=F32)


def dot_exact_left(a, v):
    n = v.shape[1]
    both = mm(a, jnp.concatenate(split2(v), axis=1))
    return both[:, :n] + both[:, n:]


def dot_exact_right(v, b):
    m = v.shape[0]
    both = mm(jnp.concatenate(split2(v), axis=0), b)
    return both[:m] + both[m:]


def dot3(a, b, trans=False):
    m = a.shape[0]
    ah, al = split2(a)
    bh, bl = split2(b)
    both = mm(jnp.concatenate([ah, al], axis=0), bh, trans)
    return both[:m] + (both[m:] + mm(ah, bl, trans))


def iota(shape, dim):
    return lax.broadcasted_iota(jnp.int32, shape, dim)


def spread_recip(pivot, row, seg):
    lane = iota((BASE, BLK), 1)
    left = jnp.where(lane % BASE == iota((BASE, BLK), 0), pivot, 0.0)
    same = jnp.where(row // BASE == seg, 1.0, 0.0).astype(BF16)
    a, rest = split2(left)
    b = rest
    c = (left - a.astype(F32) - b.astype(F32)).astype(BF16)
    got = mm(jnp.concatenate([a, b, c], axis=0), same)
    return 1.0 / (got[:BASE] + got[BASE : 2 * BASE] + got[2 * BASE :])


def invert_blocks(low, pivot):
    count = len(low)
    row, lane = iota((BLK, BLK), 0), iota((BLK, BLK), 1)
    seg = lane // BASE
    recip = [spread_recip(p, row, seg) for p in pivot]
    packed = []
    for blk in low:
        strict = jnp.where(row > lane, blk, 0.0)
        part = strict[:BASE]
        for s in range(1, BLK // BASE):
            part = jnp.where(seg[:BASE] == s, strict[s * BASE : (s + 1) * BASE], part)
        packed.append(part)
    packed = jnp.concatenate(packed, axis=0).astype(BF16)
    pick = row - seg * BASE
    one = jnp.where(row[:BASE] == lane[:BASE] % BASE, 1.0, 0.0).astype(F32)
    r = [one] * count
    for i in range(BASE - 1):
        if i % 2 == 0:
            two = jnp.concatenate([jnp.where(pick == i + j, 1.0, 0.0) for j in range(2)], axis=1).astype(BF16)
            two = mm(packed, two)
        spread = two[:, i % 2 * BLK : (i % 2 + 1) * BLK]
        top = (i + 1) // 8 * 8
        for k in range(count):
            x = r[k][i : i + 1] * recip[k][i : i + 1]
            tail = r[k][top:] - spread[k * BASE + top : (k + 1) * BASE] * x
            r[k] = jnp.concatenate([r[k][:top], tail], axis=0) if top else tail
    out = []
    for k in range(count):
        x = r[k] * recip[k]
        out.append(jnp.where(row // BASE == seg, jnp.concatenate([x] * (BLK // BASE), axis=0), 0.0))
    size = BASE
    while size < BLK:
        off = (row // size > lane // size) & (row // (2 * size) == lane // (2 * size))
        half = [dot_exact_right(x, jnp.where(off, blk, 0.0).astype(BF16)) for x, blk in zip(out, low)]
        out = [x - dot3(h, x) for x, h in zip(out, half)]
        size *= 2
    return out


def join_blocks(first, second, low):
    off = -dot3(second, dot_exact_left(low, first))
    top = jnp.concatenate([first, jnp.zeros_like(first)], axis=1)
    return jnp.concatenate([top, jnp.concatenate([off, second], axis=1)], axis=0)


def substitute(inverse, upper, right):
    xs = []
    for j, inv in enumerate(inverse):
        r = right[:, j * BIG : (j + 1) * BIG]
        if j:
            r = r - dot_exact_right(jnp.concatenate(xs, axis=1), upper(j * BIG, j))
        xs.append(dot3(r, inv, trans=True))
    return jnp.concatenate(xs, axis=1)


def power_of(largest):
    return jnp.clip(jnp.ceil(jnp.log2(largest)), -100.0, 127.0)


def scaled(x):
    blocks = x.shape[1] // BLK
    lane = iota((x.shape[0], BLK), 1) // (BLK // 2 // blocks) % blocks
    out, powers = [], jnp.zeros((x.shape[0], BLK), F32)
    for j in range(blocks):
        part = x[:, j * BLK : (j + 1) * BLK]
        power = power_of(jnp.max(jnp.abs(part), axis=1, keepdims=True))
        out.append(part * jnp.exp2(SPAN - power))
        powers = jnp.where(lane == j, power, powers)
    return jnp.concatenate(out + [powers], axis=1)


def invert_panel(panel, pivot):
    blocks = pivot.shape[1] // BLK
    at = [slice(i * BLK, (i + 1) * BLK) for i in range(blocks)]
    small = invert_blocks([panel[s, s].astype(F32).T for s in at], [pivot[:, s] for s in at])
    return [
        join_blocks(small[i], small[i + 1], panel[at[i], at[i + 1]].astype(F32).T.astype(BF16))
        for i in range(0, blocks, 2)
    ]


def scaled_rows(x):
    power = power_of(jnp.max(jnp.abs(x), axis=0, keepdims=True))
    return jnp.concatenate([x * jnp.exp2(SPAN - power), jnp.broadcast_to(power, (8, x.shape[1]))], axis=0)


def assemble(panel_ref, own_ref, other_ref):
    core = lax.axis_index("c")
    groups, count, w, _ = own_ref.shape
    for k in range(count):
        into = panel_ref.at[k]
        for g in range(groups):
            into[pl.ds(pl.multiple_of((2 * g + core) * w, w), w)] = own_ref[g, k]
            into[pl.ds(pl.multiple_of((2 * g + 1 - core) * w, w), w)] = other_ref[g, k]


def first_kernel(cols_ref, pivot_ref, right_ref, x_ref, hop_ref, panel_ref):
    cores, groups, w, _ = cols_ref.shape
    for g in range(groups):
        for c in range(cores):
            at = (cores * g + c) * w
            panel_ref[at : at + w] = cols_ref[c, g]

    @pl.when(lax.axis_index(ROW) == 0)
    def _():
        inverse = invert_panel(panel_ref, pivot_ref[0:1])
        x = substitute(inverse, lambda n, j: panel_ref[:n, j * BIG : (j + 1) * BIG], right_ref[...].T)
        x_ref[...] = x
        hop_ref[...] = scaled_rows(x)


def invert_kernel(panel_ref, pivot_ref, right_ref, inv_ref, turned_ref):
    @pl.when(lax.axis_index(ROW) == 1)
    def _():
        turned_ref[...] = right_ref[...].T
        for i, inv in enumerate(invert_panel(panel_ref, pivot_ref[1:2])):
            inv_ref[i] = inv


def second_kernel(
    got_ref, own_ref, other_ref, panel_ref, inv_ref, turned_ref, x_ref, out_ref, out_sent_ref, low_ref
):
    me = lax.axis_index(ROW)

    @pl.when(me == 0)
    def _():
        out_ref[...] = x_ref[...]
        out_sent_ref[...] = scaled(x_ref[...])

    @pl.when(me == 1)
    def _():
        inverse = [inv_ref[i] for i in range(inv_ref.shape[0])]
        x = got_ref[:-8] * jnp.exp2(got_ref[-8:-7] - SPAN)
        assemble(low_ref, own_ref, other_ref)
        right = turned_ref[...] - dot_exact_right(x, low_ref[0])
        x = substitute(inverse, lambda n, j: panel_ref[:n, j * BIG : (j + 1) * BIG], right)
        out_ref[...] = x
        out_sent_ref[...] = scaled(x)


def last_kernel(own_ref, other_ref, pieces_ref, x_ref, right_ref, out_ref, panel_ref):
    count, width, _ = panel_ref.shape
    columns = x_ref.shape[0]
    me = lax.axis_index(ROW)

    @pl.when(me < count)
    def _():
        out_ref[...] = x_ref[...].T

    @pl.when(me >= count)
    def _():
        assemble(panel_ref, own_ref, other_ref)
        got = pieces_ref[...].reshape(columns, count * width + BLK)
        update = 0.0
        for k in range(count):
            parts = []
            for j in range(width // BLK):
                at = k * width + j * BLK
                lane = count * width + at * BLK // (count * width)
                power = got[:, lane : lane + 1]
                parts.append(got[:, at : at + BLK] * jnp.exp2(power - SPAN))
            update = update + dot_exact_right(jnp.concatenate(parts, axis=1), panel_ref[k])
        out_ref[...] = right_ref[...] - update.T


def on_chip(kernel, out_shape, n_in, scratch=()):
    vmem = pl.BlockSpec(memory_space=pltpu.VMEM)
    return pl.pallas_call(
        kernel,
        out_shape=out_shape,
        in_specs=[vmem] * n_in,
        out_specs=jax.tree.map(lambda _: vmem, out_shape),
        scratch_shapes=list(scratch),
        compiler_params=pltpu.CompilerParams(vmem_limit_bytes=24 * 1024 * 1024),
    )


def same_to_all(piece, axes):
    count = lax.axis_size(axes)
    return lax.all_to_all(jnp.broadcast_to(piece[None], (count, *piece.shape)), axes, 0, 0, tiled=True)


def whole(factor, pivots, right):
    count, rows, w = factor.shape
    width = pivots.shape[1]
    columns = right.shape[1]
    n = lax.axis_size(ROW)

    piece = jnp.swapaxes(factor, 1, 2)
    near = same_to_all(piece, "zl")
    own = same_to_all(near, "x").reshape(-1, count, w, rows)
    swap = [(2 * r + c, 2 * r + 1 - c) for r in range(count, n) for c in (0, 1)]
    other_late = lax.ppermute(own, ROW + ("c",), swap)
    solved = (jax.ShapeDtypeStruct((columns, width), F32), jax.ShapeDtypeStruct((columns, width + BLK), F32))

    def solve(own, pivots, right):
        me = lax.axis_index(ROW)
        mine = lax.dynamic_index_in_dim(own, me, 1, False)
        rest = lax.dynamic_slice_in_dim(own, 1 - me, 1, 1)
        both = lax.all_gather(mine, "c")
        other = jax.ShapeDtypeStruct((columns + 8, width), F32), jax.ShapeDtypeStruct((width, rows), BF16)
        kept = (jax.ShapeDtypeStruct((width // BIG, BIG, BIG), F32), jax.ShapeDtypeStruct((columns, width), F32))
        x, hop, panel = on_chip(first_kernel, solved[:1] + other, 3)(both, pivots, right)
        got = lax.ppermute(hop.astype(jnp.float16), ROW, [(0, 1)])
        swap = [(2 * r + c, 2 * r + 1 - c) for r in range(count) for c in (0, 1)]
        low = lax.ppermute(rest, ROW + ("c",), swap)
        inverse, turned = on_chip(invert_kernel, kept, 3)(panel, pivots, right)
        scratch = [pltpu.VMEM((1, width, rows), BF16)]
        return on_chip(second_kernel, solved, 7, scratch)(
            got.astype(F32), rest, low, panel, inverse, turned, x
        )

    def skip(own, pivots, right):
        return on_chip(lambda *refs: None, solved, 1)(right)

    x, sent = lax.cond(lax.axis_index(ROW) < count, solve, skip, own, pivots, right)
    sent = sent.astype(jnp.float16).reshape(n, columns // n, width + BLK)
    mine = lax.all_to_all(sent, ROW, 0, 0, tiled=True)[:count]
    share = BLK // count
    power = [mine[k, :, width + k * share : width + (k + 1) * share] for k in range(count)]
    mine = jnp.concatenate([mine[k, :, :width] for k in range(count)] + power, axis=1)
    pieces = same_to_all(mine, ROW).astype(F32)
    scratch = [pltpu.VMEM((count, width, rows), BF16)]
    out = jax.ShapeDtypeStruct((rows, columns), F32)
    return on_chip(last_kernel, out, 5, scratch)(own, other_late, pieces, x, right)


def solution(mesh):
    ids = mesh.devices
    shape = (2, ids.shape[0] // 4, 2, ids.shape[1] // 8, 4, 2)
    split = Mesh(ids.reshape(shape), ROW + RHS)
    return jax.shard_map(
        whole,
        mesh=split,
        in_specs=(P(None, ROW, RHS), P(), P(ROW, RHS)),
        out_specs=P(ROW, RHS),
        check_vma=False,
    )
```

```python
import jax
import jax.numpy as jnp
from jax import lax
from jax.experimental import pallas as pl
from jax.experimental.pallas import tpu as pltpu
from jax.sharding import Mesh
from jax.sharding import PartitionSpec as P


ROW = ("zh", "yh", "yl")
RHS = ("x", "zl", "c")
F32, BF16 = jnp.float32, jnp.bfloat16
BASE, BLK, BIG = 32, 128, 256
SPAN = 14.0


def split2(v):
    hi = v.astype(BF16)
    lo = (v - hi.astype(F32)).astype(BF16)
    return hi, lo


def mm(a, b, trans=False):
    return lax.dot_general(a, b, (((1,), (1 if trans else 0,)), ((), ())), preferred_element_type=F32)


def dot_exact_right(v, b):
    m = v.shape[0]
    both = mm(jnp.concatenate(split2(v), axis=0), b)
    return both[:m] + both[m:]


def dot3(a, b, trans=False):
    m = a.shape[0]
    ah, al = split2(a)
    bh, bl = split2(b)
    both = mm(jnp.concatenate([ah, al], axis=0), bh, trans)
    return both[:m] + (both[m:] + mm(ah, bl, trans))


def deep_left(a, v):
    return mm(jnp.concatenate([a, a], axis=1), jnp.concatenate(split2(v), axis=0))


def deep_right(v, b):
    return mm(jnp.concatenate(split2(v), axis=1), jnp.concatenate([b, b], axis=0))


def deep3(a, b):
    ah, al = split2(a)
    bh, bl = split2(b)
    return mm(jnp.concatenate([ah, al, ah], axis=1), jnp.concatenate([bh, bh, bl], axis=0))


def iota(shape, dim):
    return lax.broadcasted_iota(jnp.int32, shape, dim)


def spread_recip(pivot, row, seg):
    lane = iota((BASE, BLK), 1)
    left = jnp.where(lane % BASE == iota((BASE, BLK), 0), pivot, 0.0)
    same = jnp.where(row // BASE == seg, 1.0, 0.0).astype(BF16)
    a, rest = split2(left)
    b = rest
    c = (left - a.astype(F32) - b.astype(F32)).astype(BF16)
    got = mm(jnp.concatenate([a, b, c], axis=0), same)
    return 1.0 / (got[:BASE] + got[BASE : 2 * BASE] + got[2 * BASE :])


def invert_blocks(low, pivot):
    count = len(low)
    row, lane = iota((BLK, BLK), 0), iota((BLK, BLK), 1)
    seg = lane // BASE
    recip = [spread_recip(p, row, seg) for p in pivot]
    packed = []
    for blk in low:
        strict = jnp.where(row > lane, blk, 0.0)
        part = strict[:BASE]
        for s in range(1, BLK // BASE):
            part = jnp.where(seg[:BASE] == s, strict[s * BASE : (s + 1) * BASE], part)
        packed.append(part)
    packed = jnp.concatenate(packed, axis=0).astype(BF16)
    pick = row - seg * BASE
    one = jnp.where(row[:BASE] == lane[:BASE] % BASE, 1.0, 0.0).astype(F32)
    r = [one] * count
    for i in range(BASE - 1):
        if i % 2 == 0:
            two = jnp.concatenate([jnp.where(pick == i + j, 1.0, 0.0) for j in range(2)], axis=1).astype(BF16)
            two = mm(packed, two)
        spread = two[:, i % 2 * BLK : (i % 2 + 1) * BLK]
        top = (i + 1) // 8 * 8
        for k in range(count):
            x = r[k][i : i + 1] * recip[k][i : i + 1]
            tail = r[k][top:] - spread[k * BASE + top : (k + 1) * BASE] * x
            r[k] = jnp.concatenate([r[k][:top], tail], axis=0) if top else tail
    out = []
    for k in range(count):
        x = r[k] * recip[k]
        out.append(jnp.where(row // BASE == seg, jnp.concatenate([x] * (BLK // BASE), axis=0), 0.0))
    size = BASE
    while size < BLK:
        off = (row // size > lane // size) & (row // (2 * size) == lane // (2 * size))
        half = [deep_right(x, jnp.where(off, blk, 0.0).astype(BF16)) for x, blk in zip(out, low)]
        out = [x - deep3(h, x) for x, h in zip(out, half)]
        size *= 2
    return out


def join_blocks(first, second, low):
    off = -deep3(second, deep_left(low, first))
    top = jnp.concatenate([first, jnp.zeros_like(first)], axis=1)
    return jnp.concatenate([top, jnp.concatenate([off, second], axis=1)], axis=0)


def substitute(inverse, upper, right):
    xs = []
    for j, inv in enumerate(inverse):
        r = right[:, j * BIG : (j + 1) * BIG]
        if j:
            r = r - dot_exact_right(jnp.concatenate(xs, axis=1), upper(j * BIG, j))
        xs.append(dot3(r, inv, trans=True))
    return jnp.concatenate(xs, axis=1)


def power_of(largest):
    return jnp.clip(jnp.ceil(jnp.log2(largest)), -100.0, 127.0)


def scaled(x):
    blocks = x.shape[1] // BLK
    lane = iota((x.shape[0], BLK), 1) // (BLK // 2 // blocks) % blocks
    out, powers = [], jnp.zeros((x.shape[0], BLK), F32)
    for j in range(blocks):
        part = x[:, j * BLK : (j + 1) * BLK]
        power = power_of(jnp.max(jnp.abs(part), axis=1, keepdims=True))
        out.append(part * jnp.exp2(SPAN - power))
        powers = jnp.where(lane == j, power, powers)
    return jnp.concatenate(out + [powers], axis=1)


def invert_panel(panel, pivot):
    blocks = pivot.shape[1] // BLK
    at = [slice(i * BLK, (i + 1) * BLK) for i in range(blocks)]
    small = invert_blocks([panel[s, s].astype(F32).T for s in at], [pivot[:, s] for s in at])
    return [
        join_blocks(small[i], small[i + 1], panel[at[i], at[i + 1]].astype(F32).T.astype(BF16))
        for i in range(0, blocks, 2)
    ]


def scaled_rows(x):
    power = power_of(jnp.max(jnp.abs(x), axis=0, keepdims=True))
    return jnp.concatenate([x * jnp.exp2(SPAN - power), jnp.broadcast_to(power, (8, x.shape[1]))], axis=0)


def assemble(panel_ref, own_ref, other_ref):
    core = lax.axis_index("c")
    groups, count, w, _ = own_ref.shape
    for k in range(count):
        into = panel_ref.at[k]
        for g in range(groups):
            into[pl.ds(pl.multiple_of((2 * g + core) * w, w), w)] = own_ref[g, k]
            into[pl.ds(pl.multiple_of((2 * g + 1 - core) * w, w), w)] = other_ref[g, k]


def first_kernel(cols_ref, pivot_ref, right_ref, x_ref, hop_ref, panel_ref):
    cores, groups, w, _ = cols_ref.shape
    for g in range(groups):
        for c in range(cores):
            at = (cores * g + c) * w
            panel_ref[at : at + w] = cols_ref[c, g]

    @pl.when(lax.axis_index(ROW) == 0)
    def _():
        inverse = invert_panel(panel_ref, pivot_ref[0:1])
        x = substitute(inverse, lambda n, j: panel_ref[:n, j * BIG : (j + 1) * BIG], right_ref[...].T)
        x_ref[...] = x
        hop_ref[...] = scaled_rows(x)


def invert_kernel(panel_ref, pivot_ref, right_ref, inv_ref, turned_ref):
    @pl.when(lax.axis_index(ROW) == 1)
    def _():
        turned_ref[...] = right_ref[...].T
        for i, inv in enumerate(invert_panel(panel_ref, pivot_ref[1:2])):
            inv_ref[i] = inv


def second_kernel(
    got_ref, own_ref, other_ref, panel_ref, inv_ref, turned_ref, x_ref, out_ref, out_sent_ref, low_ref
):
    me = lax.axis_index(ROW)

    @pl.when(me == 0)
    def _():
        out_ref[...] = x_ref[...]
        out_sent_ref[...] = scaled(x_ref[...])

    @pl.when(me == 1)
    def _():
        inverse = [inv_ref[i] for i in range(inv_ref.shape[0])]
        x = got_ref[:-8] * jnp.exp2(got_ref[-8:-7] - SPAN)
        assemble(low_ref, own_ref, other_ref)
        right = turned_ref[...] - dot_exact_right(x, low_ref[0])
        x = substitute(inverse, lambda n, j: panel_ref[:n, j * BIG : (j + 1) * BIG], right)
        out_ref[...] = x
        out_sent_ref[...] = scaled(x)


def last_kernel(own_ref, other_ref, pieces_ref, x_ref, right_ref, out_ref, panel_ref):
    count, width, _ = panel_ref.shape
    columns = x_ref.shape[0]
    me = lax.axis_index(ROW)

    @pl.when(me < count)
    def _():
        out_ref[...] = x_ref[...].T

    @pl.when(me >= count)
    def _():
        assemble(panel_ref, own_ref, other_ref)
        got = pieces_ref[...].reshape(columns, count * width + BLK)
        update = 0.0
        for k in range(count):
            parts = []
            for j in range(width // BLK):
                at = k * width + j * BLK
                lane = count * width + at * BLK // (count * width)
                power = got[:, lane : lane + 1]
                parts.append(got[:, at : at + BLK] * jnp.exp2(power - SPAN))
            update = update + dot_exact_right(jnp.concatenate(parts, axis=1), panel_ref[k])
        out_ref[...] = right_ref[...] - update.T


def on_chip(kernel, out_shape, n_in, scratch=()):
    vmem = pl.BlockSpec(memory_space=pltpu.VMEM)
    return pl.pallas_call(
        kernel,
        out_shape=out_shape,
        in_specs=[vmem] * n_in,
        out_specs=jax.tree.map(lambda _: vmem, out_shape),
        scratch_shapes=list(scratch),
        compiler_params=pltpu.CompilerParams(vmem_limit_bytes=24 * 1024 * 1024),
    )


def same_to_all(piece, axes):
    count = lax.axis_size(axes)
    return lax.all_to_all(jnp.broadcast_to(piece[None], (count, *piece.shape)), axes, 0, 0, tiled=True)


def whole(factor, pivots, right):
    count, rows, w = factor.shape
    width = pivots.shape[1]
    columns = right.shape[1]
    n = lax.axis_size(ROW)

    piece = jnp.swapaxes(factor, 1, 2)
    near = same_to_all(piece, "zl")
    own = same_to_all(near, "x").reshape(-1, count, w, rows)
    swap = [(2 * r + c, 2 * r + 1 - c) for r in range(count, n) for c in (0, 1)]
    other_late = lax.ppermute(own, ROW + ("c",), swap)
    solved = (jax.ShapeDtypeStruct((columns, width), F32), jax.ShapeDtypeStruct((columns, width + BLK), F32))

    def solve(own, pivots, right):
        me = lax.axis_index(ROW)
        mine = lax.dynamic_index_in_dim(own, me, 1, False)
        rest = lax.dynamic_slice_in_dim(own, 1 - me, 1, 1)
        both = lax.all_gather(mine, "c")
        other = jax.ShapeDtypeStruct((columns + 8, width), F32), jax.ShapeDtypeStruct((width, rows), BF16)
        kept = (jax.ShapeDtypeStruct((width // BIG, BIG, BIG), F32), jax.ShapeDtypeStruct((columns, width), F32))
        x, hop, panel = on_chip(first_kernel, solved[:1] + other, 3)(both, pivots, right)
        got = lax.ppermute(hop.astype(jnp.float16), ROW, [(0, 1)])
        swap = [(2 * r + c, 2 * r + 1 - c) for r in range(count) for c in (0, 1)]
        low = lax.ppermute(rest, ROW + ("c",), swap)
        inverse, turned = on_chip(invert_kernel, kept, 3)(panel, pivots, right)
        scratch = [pltpu.VMEM((1, width, rows), BF16)]
        return on_chip(second_kernel, solved, 7, scratch)(
            got.astype(F32), rest, low, panel, inverse, turned, x
        )

    def skip(own, pivots, right):
        return on_chip(lambda *refs: None, solved, 1)(right)

    x, sent = lax.cond(lax.axis_index(ROW) < count, solve, skip, own, pivots, right)
    sent = sent.astype(jnp.float16).reshape(n, columns // n, width + BLK)
    mine = lax.all_to_all(sent, ROW, 0, 0, tiled=True)[:count]
    share = BLK // count
    power = [mine[k, :, width + k * share : width + (k + 1) * share] for k in range(count)]
    mine = jnp.concatenate([mine[k, :, :width] for k in range(count)] + power, axis=1)
    pieces = same_to_all(mine, ROW).astype(F32)
    scratch = [pltpu.VMEM((count, width, rows), BF16)]
    out = jax.ShapeDtypeStruct((rows, columns), F32)
    return on_chip(last_kernel, out, 5, scratch)(own, other_late, pieces, x, right)


def solution(mesh):
    ids = mesh.devices
    shape = (2, ids.shape[0] // 4, 2, ids.shape[1] // 8, 4, 2)
    split = Mesh(ids.reshape(shape), ROW + RHS)
    return jax.shard_map(
        whole,
        mesh=split,
        in_specs=(P(None, ROW, RHS), P(), P(ROW, RHS)),
        out_specs=P(ROW, RHS),
        check_vma=False,
    )
```
